32 devices in a mesh: seq: 4 (over y, core), head: 8 (over z, x).
Axes of the slice: x: 2, y: 2, z: 4, core: 2. Of those that a mesh axis runs over, the one named last changes fastest.
Arguments:
- query_rows: float32 [2, 8192, 1024], P(None, 'seq', 'head'), may hold values from -0.5 to 0.5
- key_rows: float32 [2, 8192, 1024], P(None, 'seq', 'head'), may hold values from -6 to 6
- value_rows: float32 [2, 8192, 1024], P(None, 'seq', 'head'), may hold values from -6 to 6
- cotangent: float32 [2, 8192, 1024], P(None, 'seq', 'head'), may hold values from -6 to 6
- selector: int32 [2, 8, 8192], P(None, 'head', 'seq'), may hold values from 0 to 15
- level_table: float32 [16, 3], replicated, may hold values from 0.05 to 1
- span_length: int32 [2, 4], P(None, 'seq'), may hold values from 1024 to 2048
- norm_gain: float32 [1024], P('head'), may hold values from 0.1 to 1.9
Outputs:
- attended: float32 [2, 8192, 1024], P(None, 'seq', 'head')
- state_gradient: float32 [2, 4, 128, 1024], P(None, 'seq', None, 'head')
The draws below stay inside these ranges and needn't reach their ends.
Inputs may be any that keep to these rules, and one draw needn't show every extreme that they name: Keys at positions span_length and later of a block are padding.
All inputs are finite; a program needn't handle non-finite values.
Results may differ from the reference program's by a relative error of at most 0.0001.
Values sent between devices are 32-bit elements; how exact they have to be, the bound alone decides.
No kernel may reach another device: no remote copies, remote signals or barrier semaphores. Data moves between devices by JAX's collectives and lax.ppermute only.
A program may use at most 128 MiB of HBM per device.

```python
import math
import jax
import jax.numpy as jnp
from jax import lax

DH = 128
TOK_DEV = 2048
BATCH = 2
CHOICES = 16
HEADS = 8
SEQ_BITS = 2
LEVELS = 3
TOKENS = 8192
N_SEQ = 4


def set_ends(result, own_key, low, largest):
    spot = [jax.random.randint(jax.random.fold_in(own_key, axis), (), 0, length) for axis, length in enumerate(result.shape)]
    main_axis = result.shape.index(max(result.shape))
    next_to = spot[:main_axis] + [(spot[main_axis] + 1) % result.shape[main_axis]] + spot[main_axis + 1:]
    return result.at[tuple(spot)].set(low).at[tuple(next_to)].set(largest)


def block_levels(stream_key, extent, cuts, least, largest):
    gain = 1.0
    for dim, parts in cuts:
        heights = jax.random.uniform(jax.random.fold_in(jax.random.fold_in(stream_key, 6), dim), (parts,), jnp.float32, least / len(cuts), largest / len(cuts))
        gain = gain * jnp.repeat(jnp.exp(heights), extent[dim] // parts).reshape((-1,) + (1,) * (len(extent) - 1 - dim))
    return gain


def centred(key, dims, deviation, reach, cuts=(), dtype=jnp.bfloat16):
    loudness = block_levels(key, dims, cuts, -0.22, 0.18) if cuts else 1.0
    drawn = jax.random.normal(key, dims, jnp.float32) * deviation * loudness
    return jnp.minimum(jnp.maximum(drawn, -reach), reach).astype(dtype)


def setup_inputs(seed: int = 0) -> dict:
    splits = jax.random.split(jax.random.key(seed), 9)
    query_rows = centred(splits[0], (BATCH, TOKENS, HEADS * DH), DH ** -0.5, 0.5, ((1, 4), (2, 8)), jnp.float32)
    key_rows = centred(splits[1], (BATCH, TOKENS, HEADS * DH), 1.0, 6.0, ((1, 4), (2, 8)), jnp.float32)
    value_rows = centred(splits[2], (BATCH, TOKENS, HEADS * DH), 1.0, 6.0, ((1, 4), (2, 8)), jnp.float32)
    cotangent = centred(splits[3], (BATCH, TOKENS, HEADS * DH), 1.0, 6.0, ((1, 4), (2, 8)), jnp.float32)
    selector = set_ends(jax.random.randint(splits[4], (BATCH, HEADS, TOKENS), 0, CHOICES), jax.random.fold_in(splits[4], 1), 0, CHOICES - 1).astype(jnp.int32)
    level_table = jnp.clip(jnp.exp(jax.random.uniform(splits[5], (CHOICES, LEVELS), jnp.float32, math.log(0.05), math.log(1.0))), 0.05, 1.0)
    span_length = set_ends(jax.random.randint(splits[6], (BATCH, N_SEQ), TOK_DEV // 2, TOK_DEV + 1), jax.random.fold_in(splits[6], 1), TOK_DEV // 2, TOK_DEV).astype(jnp.int32)
    norm_gain = jnp.clip(1.0 + 0.18 * jax.random.normal(splits[7], (HEADS * DH,), jnp.float32), 0.1, 1.9)
    return dict(query_rows=query_rows, key_rows=key_rows, value_rows=value_rows, cotangent=cotangent, selector=selector, level_table=level_table, span_length=span_length, norm_gain=norm_gain)


epsilon = 1e-06

def reference(query_rows, key_rows, value_rows, cotangent, selector, level_table, span_length, norm_gain):
    highest = lax.Precision.HIGHEST
    shape_five = (BATCH, N_SEQ, TOK_DEV, HEADS, DH)
    queries = query_rows.reshape(shape_five)
    values = value_rows.reshape(shape_five)
    weight = level_table[selector].reshape(BATCH, HEADS, N_SEQ, TOK_DEV, LEVELS).transpose(0, 2, 3, 1, 4)
    position = jnp.arange(TOK_DEV)
    valid = (position[None, None, :] < span_length[:, :, None]).astype(jnp.float32)
    live_keys = key_rows.reshape(shape_five) * valid[..., None, None]
    state = jnp.einsum('bjshd,bjshe->bjhde', live_keys, values, precision=highest)
    causal = position[None, :] <= position[:, None]

    def local_block(pieces):
        query_block, key_block, value_block, weight_block = pieces
        scores = jnp.einsum('thd,shd->hts', query_block, key_block, precision=highest)
        scores = jnp.where(causal[None], scores, 0.0)
        mixed = jnp.einsum('hts,she->the', scores, value_block, precision=highest)
        return mixed * weight_block[:, :, 0][:, :, None]

    def flatten(array):
        return array.reshape((BATCH * N_SEQ,) + array.shape[2:])
    local = lax.map(local_block, (flatten(queries), flatten(live_keys), flatten(values), flatten(weight)))
    combined = local.reshape(shape_five)
    device_index = jnp.arange(N_SEQ)
    members = []
    for level_bit in range(SEQ_BITS):
        reader = device_index[:, None] >> level_bit
        member = ((device_index[None, :] >> level_bit == reader ^ 1) & (reader & 1 == 1)).astype(jnp.float32)
        members.append(member)
        bucket = jnp.einsum('ij,bjhde->bihde', member, state, precision=highest)
        reads = jnp.einsum('bithd,bihde->bithe', queries, bucket, precision=highest)
        combined = combined + reads * weight[..., level_bit + 1][..., None]
    combined = combined.reshape(BATCH, TOKENS, HEADS * DH)
    full_width = HEADS * DH
    mean_square = lax.optimization_barrier(jnp.sum(combined * combined, axis=2)) / full_width
    inverse = lax.rsqrt(mean_square + epsilon)
    attended = combined * inverse[..., None] * norm_gain
    scaled = cotangent * norm_gain
    inner_sum = lax.optimization_barrier(jnp.sum(scaled * combined, axis=2))
    combined_grad = scaled * inverse[..., None] - combined * (inverse * inverse * inverse * inner_sum / full_width)[..., None]
    grad_five = combined_grad.reshape(shape_five)
    state_grad = jnp.zeros((BATCH, N_SEQ, HEADS, DH, DH), jnp.float32)
    for level_bit in range(SEQ_BITS):
        level_grad = jnp.einsum('bithd,bithe->bihde', queries * weight[..., level_bit + 1][..., None], grad_five, precision=highest)
        state_grad = state_grad + jnp.einsum('ij,bihde->bjhde', members[level_bit], level_grad, precision=highest)
    state_gradient = state_grad.transpose(0, 1, 3, 2, 4).reshape(BATCH, N_SEQ, DH, HEADS * DH)
    return (attended, state_gradient)
```

```python
import functools

import jax
import jax.numpy as jnp
from jax import lax
from jax.experimental import pallas as pl
from jax.experimental.pallas import tpu as pltpu
from jax.sharding import PartitionSpec as P

DH = 128
LANES = 128
CHUNK = 256
EPSILON = 1e-06
F32, BF16 = jnp.float32, jnp.bfloat16
NN = (((1,), (0,)), ((), ()))
NT = (((1,), (1,)), ((), ()))
VMEM = pl.BlockSpec(memory_space=pltpu.VMEM)
SMEM = pl.BlockSpec(memory_space=pltpu.SMEM)
HBM = pl.BlockSpec(memory_space=pl.ANY)


def dot(left, right, dims=NN):
    return lax.dot_general(left, right, dims, preferred_element_type=F32)


def halves(array):
    high = array.astype(BF16)
    return high, (array - high.astype(F32)).astype(BF16)


def lane_row(ref, lead, chunk):
    per = CHUNK // LANES
    return jnp.concatenate(
        [ref[lead + (pl.ds(chunk * per + part, 1), slice(None))] for part in range(per)], axis=1
    )


def state_kernel(heads, span_ref, key_ref, value_ref, key_out, value_out, prefix_out, state_out):
    groups, tokens, _ = key_ref.shape
    for group in range(groups):
        span = span_ref[group // heads, 0]
        total = jnp.zeros((DH, DH), F32)
        for chunk in range(tokens // CHUNK):
            rows = pl.ds(chunk * CHUNK, CHUNK)
            position = chunk * CHUNK + lax.broadcasted_iota(jnp.int32, (CHUNK, DH), 0)
            live = jnp.where(position < span, key_ref[group, rows, :], 0.0)
            keys = jnp.concatenate(halves(live), axis=1)
            key_out[group, rows, :] = keys
            values = jnp.concatenate(halves(value_ref[group, rows, :].T), axis=0)
            value_out[group, :, rows] = values
            prefix_out[group, chunk] = jnp.concatenate(halves(total), axis=1)
            square = dot(values, keys)
            square = square[:DH] + square[DH:]
            total = total + (square[:, :DH] + square[:, DH:])
        state_out[group] = total


def query_kernel(
    heads, table_ref, query_ref, cotangent_ref, selector_ref, gain_ref, high_out, low_out, scaled_out
):
    groups, tokens, _ = query_ref.shape
    choices, levels = table_ref.shape
    for group in range(groups):
        gain = gain_ref[pl.ds(group % heads, 1), :]
        gain = jnp.broadcast_to(gain, (DH, DH)).T
        gain = jnp.concatenate([gain] * (CHUNK // DH), axis=1)
        selector = selector_ref[group]
        weights = []
        for level in range(levels):
            weight = jnp.zeros(selector.shape, F32)
            for choice in range(choices):
                weight = jnp.where(selector == choice, table_ref[choice, level], weight)
            weights.append(weight)
        for chunk in range(tokens // CHUNK):
            rows = pl.ds(chunk * CHUNK, CHUNK)
            query = query_ref[group, rows, :].T
            for level in range(levels):
                weight = lane_row(weights[level], (), chunk) if False else jnp.concatenate(
                    [
                        weights[level][chunk * (CHUNK // LANES) + part][None, :]
                        for part in range(CHUNK // LANES)
                    ],
                    axis=1,
                )
                high, low = halves(query * weight)
                high_out[group, pl.ds(level * DH, DH), rows] = high
                low_out[group, pl.ds(level * DH, DH), rows] = low
            scaled_out[group, :, rows] = cotangent_ref[group, rows, :].T * gain


def local_kernel(key_ref, value_ref, prefix_ref, high_ref, low_ref, local_out):
    groups, tokens, _ = key_ref.shape
    causal = lax.broadcasted_iota(jnp.int32, (CHUNK, CHUNK), 0) <= lax.broadcasted_iota(
        jnp.int32, (CHUNK, CHUNK), 1
    )
    for group in range(groups):
        for chunk in range(tokens // CHUNK):
            rows = pl.ds(chunk * CHUNK, CHUNK)
            high = high_ref[group, :DH, rows]
            low = low_ref[group, :DH, rows]
            left = jnp.concatenate([key_ref[group, rows, :], prefix_ref[group, chunk]], axis=0)
            mixed = dot(left, jnp.concatenate([high, high], axis=0)) + dot(left[:, :DH], low)
            scores_high, scores_low = halves(jnp.where(causal, mixed[:CHUNK], 0.0))
            values = value_ref[group, :, rows]
            near = dot(values, scores_high)
            near = near[:DH] + near[DH:] + dot(values[:DH], scores_low)
            local_out[group, :, rows] = near + mixed[CHUNK:]


def combine_kernel(
    heads, bits_ref, local_ref, high_ref, low_ref, scaled_ref, bucket_ref, combined_out, sums_out
):
    groups, _, tokens = local_ref.shape
    levels = bucket_ref.shape[0]
    per = CHUNK // LANES
    for group in range(groups):
        buckets = []
        for level in range(levels):
            buckets.append(jnp.where(bits_ref[level] == 1, bucket_ref[level, group], 0.0))
        bucket_high, bucket_low = halves(jnp.concatenate(buckets, axis=1))
        both = jnp.concatenate([bucket_high, bucket_low], axis=0)
        for chunk in range(tokens // CHUNK):
            rows = pl.ds(chunk * CHUNK, CHUNK)
            square = dot(both, high_ref[group, DH:, rows])
            square = square[:DH] + square[DH:] + dot(bucket_high, low_ref[group, DH:, rows])
            combined = square + local_ref[group, :, rows]
            combined_out[group, :, rows] = combined
            sums = (
                jnp.sum(combined * combined, axis=0, keepdims=True),
                jnp.sum(combined * scaled_ref[group, :, rows], axis=0, keepdims=True),
            )
            for kind in range(2):
                for part in range(per):
                    spot = (kind, group // heads, pl.ds(chunk * per + part, 1))
                    row = sums[kind][:, part * LANES : (part + 1) * LANES]
                    sums_out[spot] = row if group % heads == 0 else sums_out[spot] + row


def factors(sums_ref, batch, full_width):
    inverse = lax.rsqrt(sums_ref[0, batch] / full_width + EPSILON)
    return inverse, inverse * inverse * inverse * sums_ref[1, batch] / full_width


def token_row(array, chunk):
    per = CHUNK // LANES
    return jnp.concatenate(
        [array[chunk * per + part][None, :] for part in range(per)], axis=1
    )


def gradient_kernel(
    heads, full_width, sums_ref, combined_ref, scaled_ref, high_ref, low_ref, grad_out
):
    groups, _, tokens = combined_ref.shape
    levels = grad_out.shape[0]
    for group in range(groups):
        inverse, pull = factors(sums_ref, group // heads, full_width)
        first = jnp.zeros((2 * DH, levels * DH), F32)
        second = jnp.zeros((DH, levels * DH), F32)
        for chunk in range(tokens // CHUNK):
            rows = pl.ds(chunk * CHUNK, CHUNK)
            grad = scaled_ref[group, :, rows] * token_row(inverse, chunk) - combined_ref[
                group, :, rows
            ] * token_row(pull, chunk)
            both = jnp.concatenate(halves(grad), axis=0)
            first = first + dot(both, high_ref[group, DH:, rows], NT)
            second = second + dot(both[:DH], low_ref[group, DH:, rows], NT)
        second = second + first[:DH] + first[DH:]
        for level in range(levels):
            grad_out[level, group] = second[:, level * DH : (level + 1) * DH].T


def attended_kernel(heads, full_width, sums_ref, combined_ref, gain_ref, attended_out):
    groups, _, tokens = combined_ref.shape
    for group in range(groups):
        gain = gain_ref[pl.ds(group % heads, 1), :]
        gain = jnp.broadcast_to(gain, (DH, DH)).T
        gain = jnp.concatenate([gain] * (CHUNK // DH), axis=1)
        inverse, _ = factors(sums_ref, group // heads, full_width)
        for chunk in range(tokens // CHUNK):
            rows = pl.ds(chunk * CHUNK, CHUNK)
            scaled = combined_ref[group, :, rows] * token_row(inverse, chunk) * gain
            attended_out[group, rows, :] = scaled.T


def struct(shape, dtype=F32):
    return jax.ShapeDtypeStruct(shape, dtype)


def partner(shard, axis, stride):
    return lax.ppermute(shard, axis, [(i, i ^ 1 << stride) for i in range(lax.axis_size(axis))])


def local(
    query_rows, key_rows, value_rows, cotangent, selector, level_table, span_length, norm_gain
):
    batch_count, tokens, local_width = query_rows.shape
    heads = local_width // DH
    groups = batch_count * heads
    full_width = local_width * lax.axis_size("head")
    seq_index = lax.axis_index("seq")
    level_count = lax.axis_size("seq").bit_length() - 1
    bits = jnp.stack([seq_index >> level & 1 for level in range(level_count)]).astype(jnp.int32)

    def split(rows):
        rows = rows.reshape(batch_count, tokens, heads, DH)
        return rows.transpose(0, 2, 1, 3).reshape(groups, tokens, DH)

    queries, keys, values, cotangents = map(split, (query_rows, key_rows, value_rows, cotangent))
    selectors = selector.reshape(groups, tokens // LANES, LANES)
    gains = norm_gain.reshape(heads, DH)
    chunks = tokens // CHUNK
    stacked = (level_count + 1) * DH

    key_parts, value_parts, prefixes, state = pl.pallas_call(
        functools.partial(state_kernel, heads),
        out_shape=(
            struct((groups, tokens, 2 * DH), BF16),
            struct((groups, 2 * DH, tokens), BF16),
            struct((groups, chunks, DH, 2 * DH), BF16),
            struct((groups, DH, DH)),
        ),
        in_specs=[SMEM, VMEM, VMEM],
        out_specs=(VMEM,) * 4,
        name="state",
    )(span_length, keys, values)

    buckets = []
    pending = state
    for level in range(level_count):
        received = partner(pending, "seq", level)
        buckets.append(received)
        pending = pending + received

    query_high, query_low, scaled = pl.pallas_call(
        functools.partial(query_kernel, heads),
        out_shape=(
            struct((groups, stacked, tokens), BF16),
            struct((groups, stacked, tokens), BF16),
            struct((groups, DH, tokens)),
        ),
        in_specs=[SMEM, VMEM, VMEM, VMEM, VMEM],
        out_specs=(VMEM,) * 3,
        name="query",
    )(level_table, queries, cotangents, selectors, gains)

    local_sum = pl.pallas_call(
        local_kernel,
        out_shape=struct((groups, DH, tokens)),
        in_specs=[VMEM] * 5,
        out_specs=VMEM,
        name="local",
    )(key_parts, value_parts, prefixes, query_high, query_low)

    combined, sums = pl.pallas_call(
        functools.partial(combine_kernel, heads),
        out_shape=(
            struct((groups, DH, tokens)),
            struct((2, batch_count, tokens // LANES, LANES)),
        ),
        in_specs=[SMEM] + [VMEM] * 5,
        out_specs=(VMEM,) * 2,
        name="combine",
    )(bits, local_sum, query_high, query_low, scaled, jnp.stack(buckets))

    for level in range(lax.axis_size("head").bit_length() - 1):
        sums = sums + partner(sums, "head", level)

    grads = pl.pallas_call(
        functools.partial(gradient_kernel, heads, full_width),
        out_shape=struct((level_count, groups, DH, DH)),
        in_specs=[VMEM] * 5,
        out_specs=VMEM,
        name="gradient",
    )(sums, combined, scaled, query_high, query_low)

    attended = pl.pallas_call(
        functools.partial(attended_kernel, heads, full_width),
        out_shape=struct((groups, tokens, DH)),
        in_specs=[VMEM] * 3,
        out_specs=VMEM,
        name="attended",
    )(sums, combined, gains)

    total = None
    for level in reversed(range(level_count)):
        received = partner(grads[level], "seq", level)
        lower = 1.0 - bits[level].astype(F32)
        if total is None:
            total = lower * received
        else:
            total = total + partner(total, "seq", level) + lower * received

    def merge(rows, count):
        rows = rows.reshape(batch_count, heads, count, DH)
        return rows.transpose(0, 2, 1, 3).reshape(batch_count, count, heads * DH)

    return merge(attended, tokens), merge(total, DH)[:, None]


def solution(mesh):
    return jax.shard_map(
        local,
        mesh=mesh,
        in_specs=(
            P(None, "seq", "head"),
            P(None, "seq", "head"),
            P(None, "seq", "head"),
            P(None, "seq", "head"),
            P(None, "head", "seq"),
            P(),
            P(None, "seq"),
            P("head"),
        ),
        out_specs=(P(None, "seq", "head"), P(None, "seq", None, "head")),
        check_vma=False,
    )
```

```python
import functools

import jax
import jax.numpy as jnp
from jax import lax
from jax.experimental import pallas as pl
from jax.experimental.pallas import tpu as pltpu
from jax.sharding import PartitionSpec as P

DH = 128
LANES = 128
CHUNK = 256
LOAD = 512
EPSILON = 1e-06
GRANT = 20 << 20
F32, BF16 = jnp.float32, jnp.bfloat16
NN = (((1,), (0,)), ((), ()))
NT = (((1,), (1,)), ((), ()))
VMEM = pl.BlockSpec(memory_space=pltpu.VMEM)
SMEM = pl.BlockSpec(memory_space=pltpu.SMEM)
HBM = pl.BlockSpec(memory_space=pl.ANY)


def dot(left, right, dims=NN):
    return lax.dot_general(left, right, dims, preferred_element_type=F32)


def halves(array):
    high = array.astype(BF16)
    return high, (array - high.astype(F32)).astype(BF16)


def state_kernel(
    heads, span_hbm, key_hbm, value_hbm, key_out, value_out, prefix_out, state_out, *scratch
):
    span_ref, key_ref, value_ref, span_sem, key_sems, value_sems = scratch
    groups, tokens, _ = key_hbm.shape
    span_copy = pltpu.make_async_copy(span_hbm, span_ref, span_sem)
    span_copy.start()
    copies = {}
    for group in range(groups):
        for load in range(tokens // LOAD):
            rows = pl.ds(load * LOAD, LOAD)
            copies[group, load] = (
                pltpu.make_async_copy(
                    key_hbm.at[group, rows], key_ref.at[group, rows], key_sems.at[group, load]
                ),
                pltpu.make_async_copy(
                    value_hbm.at[group, rows], value_ref.at[group, rows], value_sems.at[group, load]
                ),
            )
            for copy in copies[group, load]:
                copy.start()
    span_copy.wait()
    for group in range(groups):
        span = span_ref[group // heads]
        total = jnp.zeros((DH, DH), F32)
        for chunk in range(tokens // CHUNK):
            if chunk * CHUNK % LOAD == 0:
                for copy in copies[group, chunk * CHUNK // LOAD]:
                    copy.wait()
            rows = pl.ds(chunk * CHUNK, CHUNK)
            position = chunk * CHUNK + lax.broadcasted_iota(jnp.int32, (CHUNK, DH), 0)
            live = jnp.where(position < span, key_ref[group, rows, :], 0.0)
            keys = jnp.concatenate(halves(live), axis=1)
            key_out[group, rows, :] = keys
            values = jnp.concatenate(halves(value_ref[group, rows, :].T), axis=0)
            value_out[group, :, rows] = values
            prefix_out[group, chunk] = jnp.concatenate(halves(total), axis=1)
            square = dot(values, keys)
            square = square[:DH] + square[DH:]
            total = total + (square[:, :DH] + square[:, DH:])
        state_out[group] = total


def query_kernel(
    heads, table_ref, query_ref, cotangent_ref, selector_ref, gain_ref, high_out, low_out, scaled_out
):
    groups, tokens, _ = query_ref.shape
    levels, choices = table_ref.shape
    for group in range(groups):
        gain = gain_ref[pl.ds(group % heads, 1), :]
        gain = jnp.broadcast_to(gain, (DH, DH)).T
        gain = jnp.concatenate([gain] * (CHUNK // DH), axis=1)
        selector = selector_ref[group]
        weights = []
        for level in range(levels):
            weight = jnp.zeros(selector.shape, F32)
            for choice in range(choices):
                weight = jnp.where(selector == choice, table_ref[level, choice], weight)
            weights.append(weight)
        for chunk in range(tokens // CHUNK):
            rows = pl.ds(chunk * CHUNK, CHUNK)
            query = query_ref[group, rows, :].T
            for level in range(levels):
                high, low = halves(query * token_row(weights[level], chunk))
                high_out[group, pl.ds(level * DH, DH), rows] = high
                low_out[group, pl.ds(level * DH, DH), rows] = low
            scaled_out[group, :, rows] = cotangent_ref[group, rows, :].T * gain


def local_kernel(key_ref, value_ref, prefix_ref, high_ref, low_ref, local_out):
    groups, tokens, _ = key_ref.shape
    causal = lax.broadcasted_iota(jnp.int32, (CHUNK, CHUNK), 0) <= lax.broadcasted_iota(
        jnp.int32, (CHUNK, CHUNK), 1
    )
    for group in range(groups):
        for chunk in range(tokens // CHUNK):
            rows = pl.ds(chunk * CHUNK, CHUNK)
            high = high_ref[group, :DH, rows]
            low = low_ref[group, :DH, rows]
            left = jnp.concatenate([key_ref[group, rows, :], prefix_ref[group, chunk]], axis=0)
            mixed = dot(left, jnp.concatenate([high, high], axis=0)) + dot(left[:, :DH], low)
            scores_high, scores_low = halves(jnp.where(causal, mixed[:CHUNK], 0.0))
            values = value_ref[group, :, rows]
            near = dot(values, scores_high)
            near = near[:DH] + near[DH:] + dot(values[:DH], scores_low)
            local_out[group, :, rows] = near + mixed[CHUNK:]


def combine_kernel(
    heads, local_ref, high_ref, low_ref, scaled_ref, *refs
):
    *bucket_refs, combined_out, sums_out = refs
    groups, _, tokens = local_ref.shape
    seq_index = lax.axis_index("seq")
    per = CHUNK // LANES
    for group in range(groups):
        buckets = []
        for level, bucket_ref in enumerate(bucket_refs):
            reads = seq_index >> level & 1
            buckets.append(jnp.where(reads == 1, bucket_ref[group], 0.0))
        bucket_high, bucket_low = halves(jnp.concatenate(buckets, axis=1))
        both = jnp.concatenate([bucket_high, bucket_low], axis=0)
        for chunk in range(tokens // CHUNK):
            rows = pl.ds(chunk * CHUNK, CHUNK)
            square = dot(both, high_ref[group, DH:, rows])
            square = square[:DH] + square[DH:] + dot(bucket_high, low_ref[group, DH:, rows])
            combined = square + local_ref[group, :, rows]
            combined_out[group, :, rows] = combined
            sums = (
                jnp.sum(combined * combined, axis=0, keepdims=True),
                jnp.sum(combined * scaled_ref[group, :, rows], axis=0, keepdims=True),
            )
            for kind in range(2):
                for part in range(per):
                    spot = (kind, group // heads, pl.ds(chunk * per + part, 1))
                    row = sums[kind][:, part * LANES : (part + 1) * LANES]
                    sums_out[spot] = row if group % heads == 0 else sums_out[spot] + row


def factors(sums_ref, batch, full_width):
    inverse = lax.rsqrt(sums_ref[0, batch] / full_width + EPSILON)
    return inverse, inverse * inverse * inverse * sums_ref[1, batch] / full_width


def token_row(array, chunk):
    per = CHUNK // LANES
    return jnp.concatenate(
        [array[chunk * per + part][None, :] for part in range(per)], axis=1
    )


def gradient_kernel(
    heads, full_width, sums_ref, combined_ref, scaled_ref, high_ref, low_ref, *grad_outs
):
    groups, _, tokens = combined_ref.shape
    levels = len(grad_outs)
    for group in range(groups):
        inverse, pull = factors(sums_ref, group // heads, full_width)
        first = jnp.zeros((2 * DH, levels * DH), F32)
        second = jnp.zeros((DH, levels * DH), F32)
        for chunk in range(tokens // CHUNK):
            rows = pl.ds(chunk * CHUNK, CHUNK)
            grad = scaled_ref[group, :, rows] * token_row(inverse, chunk) - combined_ref[
                group, :, rows
            ] * token_row(pull, chunk)
            both = jnp.concatenate(halves(grad), axis=0)
            first = first + dot(both, high_ref[group, DH:, rows], NT)
            second = second + dot(both[:DH], low_ref[group, DH:, rows], NT)
        second = second + first[:DH] + first[DH:]
        for level, grad_out in enumerate(grad_outs):
            grad_out[group] = second[:, level * DH : (level + 1) * DH].T


def attended_kernel(heads, full_width, sums_ref, combined_ref, gain_ref, attended_out):
    groups, _, tokens = combined_ref.shape
    for group in range(groups):
        gain = gain_ref[pl.ds(group % heads, 1), :]
        gain = jnp.broadcast_to(gain, (DH, DH)).T
        gain = jnp.concatenate([gain] * (CHUNK // DH), axis=1)
        inverse, _ = factors(sums_ref, group // heads, full_width)
        for chunk in range(tokens // CHUNK):
            rows = pl.ds(chunk * CHUNK, CHUNK)
            scaled = combined_ref[group, :, rows] * token_row(inverse, chunk) * gain
            attended_out[group, rows, :] = scaled.T


def resident(shape, dtype=F32):
    return pltpu.VMEM(shape, dtype)


def keep(array):
    return pltpu.with_memory_space_constraint(array, pltpu.VMEM)


def leave(array):
    return pltpu.with_memory_space_constraint(array, pltpu.HBM)


def partner(shard, axis, stride):
    return lax.ppermute(shard, axis, [(i, i ^ 1 << stride) for i in range(lax.axis_size(axis))])


def local(
    query_rows, key_rows, value_rows, cotangent, selector, level_table, span_length, norm_gain
):
    batch_count, tokens, local_width = query_rows.shape
    heads = local_width // DH
    groups = batch_count * heads
    full_width = local_width * lax.axis_size("head")
    seq_index = lax.axis_index("seq")
    level_count = lax.axis_size("seq").bit_length() - 1

    def split(rows):
        rows = rows.reshape(batch_count, tokens, heads, DH)
        return rows.transpose(0, 2, 1, 3).reshape(groups, tokens, DH)

    queries, keys, values, cotangents = map(split, (query_rows, key_rows, value_rows, cotangent))
    selectors = selector.reshape(groups, tokens // LANES, LANES)
    gains = norm_gain.reshape(heads, DH)
    chunks = tokens // CHUNK
    stacked = (level_count + 1) * DH

    key_parts, value_parts, prefixes, state = pl.pallas_call(
        functools.partial(state_kernel, heads),
        out_shape=(
            resident((groups, tokens, 2 * DH), BF16),
            resident((groups, 2 * DH, tokens), BF16),
            resident((groups, chunks, DH, 2 * DH), BF16),
            resident((groups, DH, DH)),
        ),
        in_specs=[HBM, HBM, HBM],
        out_specs=(VMEM,) * 4,
        scratch_shapes=[
            pltpu.SMEM((batch_count,), jnp.int32),
            pltpu.VMEM((groups, tokens, DH), F32),
            pltpu.VMEM((groups, tokens, DH), F32),
            pltpu.SemaphoreType.DMA(()),
            pltpu.SemaphoreType.DMA((groups, tokens // LOAD)),
            pltpu.SemaphoreType.DMA((groups, tokens // LOAD)),
        ],
        name="state",
        compiler_params=pltpu.CompilerParams(vmem_limit_bytes=GRANT),
    )(*map(leave, (span_length.reshape(batch_count), keys, values)))
    state, level_table, queries, cotangents, selectors, gains = lax.optimization_barrier(
        (state, level_table, queries, cotangents, selectors, gains)
    )

    buckets = []
    pending = state
    for level in range(level_count):
        received = partner(pending, "seq", level)
        buckets.append(received)
        pending = pending + received

    query_high, query_low, scaled = pl.pallas_call(
        functools.partial(query_kernel, heads),
        out_shape=(
            resident((groups, stacked, tokens), BF16),
            resident((groups, stacked, tokens), BF16),
            resident((groups, DH, tokens)),
        ),
        in_specs=[SMEM, VMEM, VMEM, VMEM, VMEM],
        out_specs=(VMEM,) * 3,
        name="query",
        compiler_params=pltpu.CompilerParams(vmem_limit_bytes=GRANT),
    )(level_table.T, queries, cotangents, selectors, gains)

    local_sum = pl.pallas_call(
        local_kernel,
        out_shape=resident((groups, DH, tokens)),
        in_specs=[VMEM] * 5,
        out_specs=VMEM,
        name="local",
        compiler_params=pltpu.CompilerParams(vmem_limit_bytes=GRANT),
    )(*map(keep, (key_parts, value_parts, prefixes, query_high, query_low)))

    combined, sums = pl.pallas_call(
        functools.partial(combine_kernel, heads),
        out_shape=(
            resident((groups, DH, tokens)),
            resident((2, batch_count, tokens // LANES, LANES)),
        ),
        in_specs=[VMEM] * (4 + level_count),
        out_specs=(VMEM,) * 2,
        name="combine",
        compiler_params=pltpu.CompilerParams(vmem_limit_bytes=GRANT),
    )(*map(keep, (local_sum, query_high, query_low, scaled, *buckets)))

    for level in range(lax.axis_size("head").bit_length() - 1):
        sums = sums + partner(sums, "head", level)

    grads = pl.pallas_call(
        functools.partial(gradient_kernel, heads, full_width),
        out_shape=(resident((groups, DH, DH)),) * level_count,
        in_specs=[VMEM] * 5,
        out_specs=(VMEM,) * level_count,
        name="gradient",
        compiler_params=pltpu.CompilerParams(vmem_limit_bytes=GRANT),
    )(*map(keep, (sums, combined, scaled, query_high, query_low)))

    attended = pl.pallas_call(
        functools.partial(attended_kernel, heads, full_width),
        out_shape=jax.ShapeDtypeStruct((groups, tokens, DH), F32),
        in_specs=[VMEM] * 3,
        out_specs=VMEM,
        name="attended",
        compiler_params=pltpu.CompilerParams(vmem_limit_bytes=GRANT),
    )(keep(sums), keep(combined), gains)

    total = None
    for level in reversed(range(level_count)):
        received = partner(grads[level], "seq", level)
        if total is None:
            received, attended = lax.optimization_barrier((received, attended))
        lower = (1 - (seq_index >> level & 1)).astype(F32)
        if total is None:
            total = lower * received
        else:
            total = total + partner(total, "seq", level) + lower * received

    def merge(rows, count):
        rows = rows.reshape(batch_count, heads, count, DH)
        return rows.transpose(0, 2, 1, 3).reshape(batch_count, count, heads * DH)

    return merge(attended, tokens), merge(total, DH)[:, None]


def solution(mesh):
    return jax.shard_map(
        local,
        mesh=mesh,
        in_specs=(
            P(None, "seq", "head"),
            P(None, "seq", "head"),
            P(None, "seq", "head"),
            P(None, "seq", "head"),
            P(None, "head", "seq"),
            P(),
            P(None, "seq"),
            P("head"),
        ),
        out_specs=(P(None, "seq", "head"), P(None, "seq", None, "head")),
        check_vma=False,
    )
```

```python
import functools

import jax
import jax.numpy as jnp
from jax import lax
from jax.experimental import pallas as pl
from jax.experimental.pallas import tpu as pltpu
from jax.sharding import PartitionSpec as P

DH = 128
LANES = 128
CHUNK = 256
LOAD = 512
EPSILON = 1e-06
GRANT = 8 << 20
F32, BF16 = jnp.float32, jnp.bfloat16
NN = (((1,), (0,)), ((), ()))
NT = (((1,), (1,)), ((), ()))
VMEM = pl.BlockSpec(memory_space=pltpu.VMEM)
SMEM = pl.BlockSpec(memory_space=pltpu.SMEM)
HBM = pl.BlockSpec(memory_space=pl.ANY)


def dot(left, right, dims=NN):
    return lax.dot_general(left, right, dims, preferred_element_type=F32)


def halves(array):
    high = array.astype(BF16)
    return high, (array - high.astype(F32)).astype(BF16)


def chunk_states(groups, tokens, spans, key_at, value_at, outs, ready=None):
    key_out, value_out, prefix_out, state_out = outs
    spots = [(group, chunk) for group in range(groups) for chunk in range(tokens // CHUNK)]

    def prepare(group, chunk):
        if ready is not None:
            ready(group, chunk)
        rows = pl.ds(chunk * CHUNK, CHUNK)
        position = chunk * CHUNK + lax.broadcasted_iota(jnp.int32, (CHUNK, DH), 0)
        live = jnp.where(position < spans[group], key_at(group, rows), 0.0)
        key_out[group, rows, :] = jnp.concatenate(halves(live), axis=1)
        value_out[group, :, rows] = jnp.concatenate(halves(value_at(group, rows).T), axis=0)

    prepare(*spots[0])
    total = None
    for index, (group, chunk) in enumerate(spots):
        if index + 1 < len(spots):
            prepare(*spots[index + 1])
        rows = pl.ds(chunk * CHUNK, CHUNK)
        total = jnp.zeros((DH, DH), F32) if chunk == 0 else total
        prefix_out[group, chunk] = jnp.concatenate(halves(total), axis=1)
        square = dot(value_out[group, :, rows], key_out[group, rows, :])
        square = square[:DH] + square[DH:]
        total = total + (square[:, :DH] + square[:, DH:])
        if chunk == tokens // CHUNK - 1:
            state_out[group] = total


def state_kernel(heads, span_hbm, key_hbm, value_hbm, *refs):
    *outs, span_ref, key_ref, value_ref, span_sem, sems = refs
    groups, tokens, _ = key_ref.shape
    span_copy = pltpu.make_async_copy(span_hbm, span_ref, span_sem)
    span_copy.start()
    loads = {}
    for group in range(groups):
        for load in range(tokens // LOAD):
            rows = pl.ds(load * LOAD, LOAD)
            loads[group, load] = [
                pltpu.make_async_copy(
                    source.at[group, rows], target.at[group, rows], sems.at[kind, group, load]
                )
                for kind, (source, target) in enumerate(
                    ((key_hbm, key_ref), (value_hbm, value_ref))
                )
            ]
            for copy in loads[group, load]:
                copy.start()
    span_copy.wait()

    def ready(group, chunk):
        if chunk * CHUNK % LOAD == 0:
            for copy in loads[group, chunk * CHUNK // LOAD]:
                copy.wait()

    chunk_states(
        groups,
        tokens,
        [span_ref[group // heads] for group in range(groups)],
        lambda group, rows: key_ref[group, rows, :],
        lambda group, rows: value_ref[group, rows, :],
        outs,
        ready,
    )


def token_kernel(heads, table_ref, selector_ref, cotangent_ref, gain_ref, weight_out, scaled_out):
    groups, tokens, _ = cotangent_ref.shape
    levels, choices = table_ref.shape
    for group in range(groups):
        gain = gain_ref[pl.ds(group % heads, 1), :]
        for chunk in range(tokens // CHUNK):
            rows = pl.ds(chunk * CHUNK, CHUNK)
            scaled_out[group, :, rows] = (cotangent_ref[group, rows, :] * gain).T
    for group in range(groups):
        selector = selector_ref[group]
        for level in range(levels):
            weight = jnp.zeros(selector.shape, F32)
            for choice in range(choices):
                weight = jnp.where(selector == choice, table_ref[level, choice], weight)
            weight_out[level, group] = weight


def causal_halves(scores, ahead):
    strips = []
    for row in range(0, CHUNK, LANES):
        blocks = []
        for column in range(0, CHUNK, LANES):
            block = scores[row : row + LANES, column : column + LANES]
            if row == column:
                block = jnp.where(ahead, block, 0.0)
            zero = jnp.zeros(block.shape, BF16)
            blocks.append((zero, zero) if row > column else halves(block))
        strips.append([jnp.concatenate(parts, axis=1) for parts in zip(*blocks)])
    return [jnp.concatenate(parts, axis=0) for parts in zip(*strips)]


def local_kernel(weight_ref, query_ref, key_ref, value_ref, prefix_ref, *refs):
    high_out, low_out, local_out, high_own, low_own = refs
    groups, tokens, _ = query_ref.shape
    levels = weight_ref.shape[0]
    ahead = lax.broadcasted_iota(jnp.int32, (LANES, LANES), 0) <= lax.broadcasted_iota(
        jnp.int32, (LANES, LANES), 1
    )
    spots = [(group, chunk) for group in range(groups) for chunk in range(tokens // CHUNK)]

    def prepare(index):
        group, chunk = spots[index]
        rows = pl.ds(chunk * CHUNK, CHUNK)
        query = query_ref[group, rows, :].T
        high_own[index % 2], low_own[index % 2] = halves(
            query * token_row(weight_ref.at[0, group], chunk)
        )
        for level in range(1, levels):
            high, low = halves(query * token_row(weight_ref.at[level, group], chunk))
            high_out[group, pl.ds((level - 1) * DH, DH), rows] = high
            low_out[group, pl.ds((level - 1) * DH, DH), rows] = low

    prepare(0)
    for index, (group, chunk) in enumerate(spots):
        if index + 1 < len(spots):
            prepare(index + 1)
        rows = pl.ds(chunk * CHUNK, CHUNK)
        high, low = high_own[index % 2], low_own[index % 2]
        left = jnp.concatenate([key_ref[group, rows, :], prefix_ref[group, chunk]], axis=0)
        mixed = dot(left, jnp.concatenate([high, high], axis=0)) + dot(left[:, :DH], low)
        scores_high, scores_low = causal_halves(mixed[:CHUNK], ahead)
        values = value_ref[group, :, rows]
        near = dot(values, scores_high)
        near = near[:DH] + near[DH:] + dot(values[:DH], scores_low)
        local_out[group, :, rows] = near + mixed[CHUNK:]


def combine_kernel(
    heads, local_ref, high_ref, low_ref, scaled_ref, *refs
):
    *bucket_refs, combined_out, sums_out = refs
    groups, _, tokens = local_ref.shape
    seq_index = lax.axis_index("seq")
    per = CHUNK // LANES
    for group in range(groups):
        buckets = []
        for level, bucket_ref in enumerate(bucket_refs):
            reads = seq_index >> level & 1
            buckets.append(jnp.where(reads == 1, bucket_ref[group], 0.0))
        bucket_high, bucket_low = halves(jnp.concatenate(buckets, axis=1))
        both = jnp.concatenate([bucket_high, bucket_low], axis=0)
        for chunk in range(tokens // CHUNK):
            rows = pl.ds(chunk * CHUNK, CHUNK)
            square = dot(both, high_ref[group, :, rows])
            square = square[:DH] + square[DH:] + dot(bucket_high, low_ref[group, :, rows])
            combined = square + local_ref[group, :, rows]
            combined_out[group, :, rows] = combined
            sums = (
                jnp.sum(combined * combined, axis=0, keepdims=True),
                jnp.sum(combined * scaled_ref[group, :, rows], axis=0, keepdims=True),
            )
            for kind in range(2):
                for part in range(per):
                    spot = (kind, group // heads, pl.ds(chunk * per + part, 1))
                    row = sums[kind][:, part * LANES : (part + 1) * LANES]
                    sums_out[spot] = row if group % heads == 0 else sums_out[spot] + row


def factors(sums_ref, batch, full_width):
    inverse = lax.rsqrt(sums_ref[0, batch] / full_width + EPSILON)
    return inverse, inverse * inverse * inverse * sums_ref[1, batch] / full_width


def token_row(array, chunk):
    per = CHUNK // LANES
    spots = range(chunk * per, (chunk + 1) * per)
    return jnp.concatenate([array[spot : spot + 1, :] for spot in spots], axis=1)


def fold(total):
    total = total[:DH] + total[DH:]
    return (total[:, :DH] + total[:, DH:]).T


def top_gradient_kernel(
    heads, full_width, sums_ref, combined_ref, scaled_ref, high_ref, low_ref, *outs
):
    grad_out, parts_out = outs
    groups, _, tokens = combined_ref.shape
    level = high_ref.shape[1] // DH - 1
    top = pl.ds(level * DH, DH)
    reads = lax.axis_index("seq") >> level & 1
    for group in range(groups):
        inverse, pull = factors(sums_ref, group // heads, full_width)
        total = jnp.zeros((2 * DH, 2 * DH), F32)
        for chunk in range(tokens // CHUNK):
            rows = pl.ds(chunk * CHUNK, CHUNK)
            grad = scaled_ref[group, :, rows] * token_row(inverse, chunk) - combined_ref[
                group, :, rows
            ] * token_row(pull, chunk)
            both = jnp.concatenate(halves(grad), axis=0)
            parts_out[group, :, rows] = both
            weighted = jnp.concatenate([high_ref[group, top, rows], low_ref[group, top, rows]], 0)
            total = total + dot(both, weighted, NT)
        grad_out[group] = jnp.where(reads == 1, fold(total), 0.0)


def rest_gradient_kernel(parts_ref, high_ref, low_ref, *grad_outs):
    groups, _, tokens = parts_ref.shape
    for level, grad_out in enumerate(grad_outs):
        spot = pl.ds(level * DH, DH)
        reads = lax.axis_index("seq") >> level & 1
        for group in range(groups):
            total = jnp.zeros((2 * DH, 2 * DH), F32)
            for chunk in range(tokens // CHUNK):
                rows = pl.ds(chunk * CHUNK, CHUNK)
                weighted = jnp.concatenate(
                    [high_ref[group, spot, rows], low_ref[group, spot, rows]], 0
                )
                total = total + dot(parts_ref[group, :, rows], weighted, NT)
            grad_out[group] = jnp.where(reads == 1, fold(total), 0.0)


def finish_kernel(*refs):
    *part_refs, out_ref = refs
    total = part_refs[0][...]
    for part_ref in part_refs[1:]:
        total = total + part_ref[...]
    out_ref[...] = total


def attended_kernel(
    heads, full_width, sums_ref, combined_ref, gain_ref, attended_hbm, attended_ref, sems
):
    groups, _, tokens = combined_ref.shape
    copies = []
    for group in range(groups):
        gain = gain_ref[pl.ds(group % heads, 1), :]
        inverse, _ = factors(sums_ref, group // heads, full_width)
        for chunk in range(tokens // CHUNK):
            rows = pl.ds(chunk * CHUNK, CHUNK)
            scaled = combined_ref[group, :, rows] * token_row(inverse, chunk)
            attended_ref[group, rows, :] = scaled.T * gain
            if (chunk + 1) * CHUNK % LOAD == 0:
                load = (chunk + 1) * CHUNK // LOAD - 1
                rows = pl.ds(load * LOAD, LOAD)
                copies.append(
                    pltpu.make_async_copy(
                        attended_ref.at[group, rows],
                        attended_hbm.at[group, rows],
                        sems.at[group, load],
                    )
                )
                copies[-1].start()
    for copy in copies:
        copy.wait()


def resident(shape, dtype=F32):
    return pltpu.VMEM(shape, dtype)


def keep(array):
    return pltpu.with_memory_space_constraint(array, pltpu.VMEM)


def leave(array):
    return pltpu.with_memory_space_constraint(array, pltpu.HBM)


def partner(shard, axis, stride):
    return lax.ppermute(shard, axis, [(i, i ^ 1 << stride) for i in range(lax.axis_size(axis))])


def exchange(shard, axis, masks):
    size = lax.axis_size(axis)
    others = [lax.ppermute(shard, axis, [(i, i ^ mask) for i in range(size)]) for mask in masks]
    return sum(others, shard)


def body(
    query_rows, key_rows, value_rows, cotangent, selector, level_table, span_length, norm_gain
):
    batch_count, tokens, local_width = query_rows.shape
    heads = local_width // DH
    groups = batch_count * heads
    full_width = local_width * lax.axis_size("head")
    level_count = lax.axis_size("seq").bit_length() - 1

    def split(rows):
        rows = rows.reshape(batch_count, tokens, heads, DH)
        return rows.transpose(0, 2, 1, 3).reshape(groups, tokens, DH)

    queries, keys, values, cotangents = map(split, (query_rows, key_rows, value_rows, cotangent))
    selectors = selector.reshape(groups, tokens // LANES, LANES)
    gains = norm_gain.reshape(heads, DH)
    chunks = tokens // CHUNK
    stacked = level_count * DH
    call = functools.partial(
        pl.pallas_call, compiler_params=pltpu.CompilerParams(vmem_limit_bytes=GRANT)
    )

    key_parts, value_parts, prefixes, state = call(
        functools.partial(state_kernel, heads),
        out_shape=(
            resident((groups, tokens, 2 * DH), BF16),
            resident((groups, 2 * DH, tokens), BF16),
            resident((groups, chunks, DH, 2 * DH), BF16),
            resident((groups, DH, DH)),
        ),
        in_specs=[HBM] * 3,
        out_specs=(VMEM,) * 4,
        scratch_shapes=[
            pltpu.SMEM((batch_count,), jnp.int32),
            pltpu.VMEM((groups, tokens, DH), F32),
            pltpu.VMEM((groups, tokens, DH), F32),
            pltpu.SemaphoreType.DMA(()),
            pltpu.SemaphoreType.DMA((2, groups, tokens // LOAD)),
        ],
        name="state",
    )(*map(leave, (span_length.reshape(batch_count), keys, values)))
    state, queries, cotangents, gains, selectors, level_table = lax.optimization_barrier(
        (state, queries, cotangents, gains, selectors, level_table)
    )

    weights, scaled = call(
        functools.partial(token_kernel, heads),
        out_shape=(
            resident((level_count + 1, groups, tokens // LANES, LANES)),
            resident((groups, DH, tokens)),
        ),
        in_specs=[SMEM] + [VMEM] * 3,
        out_specs=(VMEM,) * 2,
        name="token",
    )(level_table.T, selectors, cotangents, gains)

    buckets = []
    pending = state
    for level in range(level_count):
        buckets.append(partner(pending, "seq", level))
        pending = pending + buckets[-1]

    weighted_high, weighted_low, local_sum = call(
        local_kernel,
        out_shape=(
            resident((groups, stacked, tokens), BF16),
            resident((groups, stacked, tokens), BF16),
            resident((groups, DH, tokens)),
        ),
        in_specs=[VMEM] * 5,
        out_specs=(VMEM,) * 3,
        scratch_shapes=[pltpu.VMEM((2, DH, CHUNK), BF16)] * 2,
        name="local",
    )(*map(keep, (weights, queries, key_parts, value_parts, prefixes)))

    combined, sums = call(
        functools.partial(combine_kernel, heads),
        out_shape=(
            resident((groups, DH, tokens)),
            resident((2, batch_count, tokens // LANES, LANES)),
        ),
        in_specs=[VMEM] * (4 + level_count),
        out_specs=(VMEM,) * 2,
        name="combine",
    )(*map(keep, (local_sum, weighted_high, weighted_low, scaled, *buckets)))

    head_bits = lax.axis_size("head").bit_length() - 1
    sums = exchange(sums, "head", range(1, 1 << min(2, head_bits)))
    for level in range(2, head_bits):
        sums = exchange(sums, "head", (1 << level,))

    top_grad, grad_parts = call(
        functools.partial(top_gradient_kernel, heads, full_width),
        out_shape=(resident((groups, DH, DH)), resident((groups, 2 * DH, tokens), BF16)),
        in_specs=[VMEM] * 5,
        out_specs=(VMEM,) * 2,
        name="top_gradient",
    )(*map(keep, (sums, combined, scaled, weighted_high, weighted_low)))
    grads = call(
        rest_gradient_kernel,
        out_shape=(resident((groups, DH, DH)),) * (level_count - 1),
        in_specs=[VMEM] * 3,
        out_specs=(VMEM,) * (level_count - 1),
        name="rest_gradient",
    )(*map(keep, (grad_parts, weighted_high, weighted_low)))

    attended = call(
        functools.partial(attended_kernel, heads, full_width),
        out_shape=jax.ShapeDtypeStruct((groups, tokens, DH), F32),
        in_specs=[VMEM] * 3,
        out_specs=HBM,
        scratch_shapes=[
            pltpu.VMEM((groups, tokens, DH), F32),
            pltpu.SemaphoreType.DMA((groups, tokens // LOAD)),
        ],
        name="attended",
    )(keep(sums), keep(combined), gains)

    total = partner(top_grad, "seq", level_count - 1)
    parts = []
    for level in reversed(range(level_count - 1)):
        total = sum(parts, total)
        received = partner(grads[level], "seq", level)
        parts = [partner(total, "seq", level), received]
    total = call(
        finish_kernel,
        out_shape=jax.ShapeDtypeStruct((groups, DH, DH), F32),
        in_specs=[VMEM] * 3,
        out_specs=VMEM,
        name="finish",
    )(*map(keep, (total, *parts)))

    def merge(rows, count):
        rows = rows.reshape(batch_count, heads, count, DH)
        return rows.transpose(0, 2, 1, 3).reshape(batch_count, count, heads * DH)

    return merge(attended, tokens), merge(total, DH)[:, None]


def solution(mesh):
    return jax.shard_map(
        body,
        mesh=mesh,
        in_specs=(
            P(None, "seq", "head"),
            P(None, "seq", "head"),
            P(None, "seq", "head"),
            P(None, "seq", "head"),
            P(None, "head", "seq"),
            P(),
            P(None, "seq"),
            P("head"),
        ),
        out_specs=(P(None, "seq", "head"), P(None, "seq", None, "head")),
        check_vma=False,
    )
```

```python
import functools

import jax
import jax.numpy as jnp
from jax import lax
from jax.experimental import pallas as pl
from jax.experimental.pallas import tpu as pltpu
from jax.sharding import PartitionSpec as P

DH = 128
LANES = 128
CHUNK = 256
LOAD = 1024
EPSILON = 1e-06
GRANT = 8 << 20
F32, BF16 = jnp.float32, jnp.bfloat16
NN = (((1,), (0,)), ((), ()))
NT = (((1,), (1,)), ((), ()))
VMEM = pl.BlockSpec(memory_space=pltpu.VMEM)
SMEM = pl.BlockSpec(memory_space=pltpu.SMEM)
HBM = pl.BlockSpec(memory_space=pl.ANY)


def dot(left, right, dims=NN):
    return lax.dot_general(left, right, dims, preferred_element_type=F32)


def halves(array):
    high = array.astype(BF16)
    return high, (array - high.astype(F32)).astype(BF16)


def chunk_states(groups, tokens, spans, key_at, value_at, outs, ready=None):
    key_out, value_out, prefix_out, state_out = outs
    spots = [(group, chunk) for group in range(groups) for chunk in range(tokens // CHUNK)]

    def prepare(group, chunk):
        if ready is not None:
            ready(group, chunk)
        rows = pl.ds(chunk * CHUNK, CHUNK)
        live = key_at(group, rows)
        if (chunk + 1) * CHUNK > tokens // 2:
            position = lax.broadcasted_iota(jnp.int32, (CHUNK, DH), 0)
            live = jnp.where(position < spans[group] - chunk * CHUNK, live, 0.0)
        key_out[group, rows, :] = jnp.concatenate(halves(live), axis=1)
        value_out[group, :, rows] = jnp.concatenate(halves(value_at(group, rows).T), axis=0)

    prepare(*spots[0])
    total = None
    for index, (group, chunk) in enumerate(spots):
        if index + 1 < len(spots):
            prepare(*spots[index + 1])
        rows = pl.ds(chunk * CHUNK, CHUNK)
        total = jnp.zeros((DH, DH), F32) if chunk == 0 else total
        prefix_out[group, chunk] = jnp.concatenate(halves(total), axis=1)
        square = dot(value_out[group, :, rows], key_out[group, rows, :])
        square = square[:DH] + square[DH:]
        total = total + (square[:, :DH] + square[:, DH:])
        if chunk == tokens // CHUNK - 1:
            state_out[group] = total


def state_kernel(heads, span_hbm, key_hbm, value_hbm, *refs):
    *outs, span_ref, key_ref, value_ref, span_sem, sems = refs
    groups, tokens, _ = key_ref.shape
    span_copy = pltpu.make_async_copy(span_hbm, span_ref, span_sem)
    span_copy.start()
    loads = {}
    for group in range(groups):
        for load in range(tokens // LOAD):
            rows = pl.ds(load * LOAD, LOAD)
            loads[group, load] = [
                pltpu.make_async_copy(
                    source.at[group, rows], target.at[group, rows], sems.at[kind, group, load]
                )
                for kind, (source, target) in enumerate(
                    ((key_hbm, key_ref), (value_hbm, value_ref))
                )
            ]
            for copy in loads[group, load]:
                copy.start()
    span_copy.wait()

    def ready(group, chunk):
        if chunk * CHUNK % LOAD == 0:
            for copy in loads[group, chunk * CHUNK // LOAD]:
                copy.wait()

    chunk_states(
        groups,
        tokens,
        [span_ref[group // heads] for group in range(groups)],
        lambda group, rows: key_ref[group, rows, :],
        lambda group, rows: value_ref[group, rows, :],
        outs,
        ready,
    )


def token_kernel(heads, table_ref, selector_ref, cotangent_ref, gain_ref, weight_out, scaled_out):
    groups, tokens, _ = cotangent_ref.shape
    levels, choices = table_ref.shape
    for group in range(groups):
        gain = gain_ref[pl.ds(group % heads, 1), :]
        for chunk in range(tokens // CHUNK):
            rows = pl.ds(chunk * CHUNK, CHUNK)
            scaled_out[group, :, rows] = (cotangent_ref[group, rows, :] * gain).T
    for group in range(groups):
        selector = selector_ref[group]
        for level in range(levels):
            weight = jnp.zeros(selector.shape, F32)
            for choice in range(choices):
                weight = jnp.where(selector == choice, table_ref[level, choice], weight)
            weight_out[level, group] = weight


def causal_halves(scores, ahead):
    strips = []
    for row in range(0, CHUNK, LANES):
        blocks = []
        for column in range(0, CHUNK, LANES):
            block = scores[row : row + LANES, column : column + LANES]
            if row == column:
                block = jnp.where(ahead, block, 0.0)
            zero = jnp.zeros(block.shape, BF16)
            blocks.append((zero, zero) if row > column else halves(block))
        strips.append([jnp.concatenate(parts, axis=1) for parts in zip(*blocks)])
    return [jnp.concatenate(parts, axis=0) for parts in zip(*strips)]


def local_kernel(weight_ref, query_ref, key_ref, value_ref, prefix_ref, *refs):
    high_out, low_out, local_out, high_own, low_own = refs
    groups, tokens, _ = query_ref.shape
    levels = weight_ref.shape[0]
    ahead = lax.broadcasted_iota(jnp.int32, (LANES, LANES), 0) <= lax.broadcasted_iota(
        jnp.int32, (LANES, LANES), 1
    )
    spots = [(group, chunk) for group in range(groups) for chunk in range(tokens // CHUNK)]

    def prepare(index):
        group, chunk = spots[index]
        rows = pl.ds(chunk * CHUNK, CHUNK)
        query = query_ref[group, rows, :].T
        high_own[index % 2], low_own[index % 2] = halves(
            query * token_row(weight_ref.at[0, group], chunk)
        )
        for level in range(1, levels):
            high, low = halves(query * token_row(weight_ref.at[level, group], chunk))
            high_out[group, pl.ds((level - 1) * DH, DH), rows] = high
            low_out[group, pl.ds((level - 1) * DH, DH), rows] = low

    prepare(0)
    for index, (group, chunk) in enumerate(spots):
        if index + 1 < len(spots):
            prepare(index + 1)
        rows = pl.ds(chunk * CHUNK, CHUNK)
        high, low = high_own[index % 2], low_own[index % 2]
        left = jnp.concatenate([key_ref[group, rows, :], prefix_ref[group, chunk]], axis=0)
        mixed = dot(left, jnp.concatenate([high, high], axis=0)) + dot(left[:, :DH], low)
        scores_high, scores_low = causal_halves(mixed[:CHUNK], ahead)
        values = value_ref[group, :, rows]
        near = dot(values, scores_high)
        near = near[:DH] + near[DH:] + dot(values[:DH], scores_low)
        local_out[group, :, rows] = near + mixed[CHUNK:]


def combine_kernel(
    heads, local_ref, high_ref, low_ref, scaled_ref, *refs
):
    *bucket_refs, combined_out, sums_out = refs
    groups, _, tokens = local_ref.shape
    seq_index = lax.axis_index("seq")
    per = CHUNK // LANES
    for group in range(groups):
        buckets = []
        for level, bucket_ref in enumerate(bucket_refs):
            reads = seq_index >> level & 1
            buckets.append(jnp.where(reads == 1, bucket_ref[group], 0.0))
        bucket_high, bucket_low = halves(jnp.concatenate(buckets, axis=1))
        both = jnp.concatenate([bucket_high, bucket_low], axis=0)
        for chunk in range(tokens // CHUNK):
            rows = pl.ds(chunk * CHUNK, CHUNK)
            square = dot(both, high_ref[group, :, rows])
            square = square[:DH] + square[DH:] + dot(bucket_high, low_ref[group, :, rows])
            combined = square + local_ref[group, :, rows]
            combined_out[group, :, rows] = combined
            sums = (
                jnp.sum(combined * combined, axis=0, keepdims=True),
                jnp.sum(combined * scaled_ref[group, :, rows], axis=0, keepdims=True),
            )
            for kind in range(2):
                for part in range(per):
                    spot = (kind, group // heads, pl.ds(chunk * per + part, 1))
                    row = sums[kind][:, part * LANES : (part + 1) * LANES]
                    sums_out[spot] = row if group % heads == 0 else sums_out[spot] + row


def factors(sums_ref, batch, full_width):
    inverse = lax.rsqrt(sums_ref[0, batch] / full_width + EPSILON)
    return inverse, inverse * inverse * inverse * sums_ref[1, batch] / full_width


def token_row(array, chunk):
    per = CHUNK // LANES
    spots = range(chunk * per, (chunk + 1) * per)
    return jnp.concatenate([array[spot : spot + 1, :] for spot in spots], axis=1)


def fold(total):
    total = total[:DH] + total[DH:]
    return (total[:, :DH] + total[:, DH:]).T


def top_gradient_kernel(
    heads, full_width, sums_ref, combined_ref, scaled_ref, high_ref, low_ref, *outs
):
    grad_out, parts_out = outs
    groups, _, tokens = combined_ref.shape
    level = high_ref.shape[1] // DH - 1
    top = pl.ds(level * DH, DH)
    reads = lax.axis_index("seq") >> level & 1
    for group in range(groups):
        inverse, pull = factors(sums_ref, group // heads, full_width)
        for chunk in range(tokens // CHUNK):
            rows = pl.ds(chunk * CHUNK, CHUNK)
            grad = scaled_ref[group, :, rows] * token_row(inverse, chunk) - combined_ref[
                group, :, rows
            ] * token_row(pull, chunk)
            parts_out[group, :, rows] = jnp.concatenate(halves(grad), axis=0)
        weighted = jnp.concatenate([high_ref[group, top, :], low_ref[group, top, :]], 0)
        total = dot(parts_out[group], weighted, NT)
        grad_out[group] = jnp.where(reads == 1, fold(total), 0.0)


def rest_gradient_kernel(parts_ref, high_ref, low_ref, *grad_outs):
    groups, _, _ = parts_ref.shape
    for level, grad_out in enumerate(grad_outs):
        spot = pl.ds(level * DH, DH)
        reads = lax.axis_index("seq") >> level & 1
        for group in range(groups):
            weighted = jnp.concatenate([high_ref[group, spot, :], low_ref[group, spot, :]], 0)
            total = dot(parts_ref[group], weighted, NT)
            grad_out[group] = jnp.where(reads == 1, fold(total), 0.0)


def finish_kernel(*refs):
    *part_refs, out_ref = refs
    total = part_refs[0][...]
    for part_ref in part_refs[1:]:
        total = total + part_ref[...]
    out_ref[...] = total


def attended_kernel(
    heads, full_width, sums_ref, combined_ref, gain_ref, attended_hbm, attended_ref, sems
):
    groups, _, tokens = combined_ref.shape
    copies = []
    for group in range(groups):
        gain = gain_ref[pl.ds(group % heads, 1), :]
        inverse, _ = factors(sums_ref, group // heads, full_width)
        for chunk in range(tokens // CHUNK):
            rows = pl.ds(chunk * CHUNK, CHUNK)
            scaled = combined_ref[group, :, rows] * token_row(inverse, chunk)
            attended_ref[group, rows, :] = scaled.T * gain
            if (chunk + 1) * CHUNK % LOAD == 0:
                load = (chunk + 1) * CHUNK // LOAD - 1
                rows = pl.ds(load * LOAD, LOAD)
                copies.append(
                    pltpu.make_async_copy(
                        attended_ref.at[group, rows],
                        attended_hbm.at[group, rows],
                        sems.at[group, load],
                    )
                )
                copies[-1].start()
    for copy in copies:
        copy.wait()


def resident(shape, dtype=F32):
    return pltpu.VMEM(shape, dtype)


def keep(array):
    return pltpu.with_memory_space_constraint(array, pltpu.VMEM)


def leave(array):
    return pltpu.with_memory_space_constraint(array, pltpu.HBM)


def partner(shard, axis, stride):
    return lax.ppermute(shard, axis, [(i, i ^ 1 << stride) for i in range(lax.axis_size(axis))])


def exchange(shard, axis, masks):
    size = lax.axis_size(axis)
    others = [lax.ppermute(shard, axis, [(i, i ^ mask) for i in range(size)]) for mask in masks]
    return sum(others, shard)


def body(
    query_rows, key_rows, value_rows, cotangent, selector, level_table, span_length, norm_gain
):
    batch_count, tokens, local_width = query_rows.shape
    heads = local_width // DH
    groups = batch_count * heads
    full_width = local_width * lax.axis_size("head")
    level_count = lax.axis_size("seq").bit_length() - 1

    def split(rows):
        rows = rows.reshape(batch_count, tokens, heads, DH)
        return rows.transpose(0, 2, 1, 3).reshape(groups, tokens, DH)

    queries, keys, values, cotangents = map(split, (query_rows, key_rows, value_rows, cotangent))
    selectors = selector.reshape(groups, tokens // LANES, LANES)
    gains = norm_gain.reshape(heads, DH)
    chunks = tokens // CHUNK
    stacked = level_count * DH
    call = functools.partial(
        pl.pallas_call, compiler_params=pltpu.CompilerParams(vmem_limit_bytes=GRANT)
    )

    key_parts, value_parts, prefixes, state = call(
        functools.partial(state_kernel, heads),
        out_shape=(
            resident((groups, tokens, 2 * DH), BF16),
            resident((groups, 2 * DH, tokens), BF16),
            resident((groups, chunks, DH, 2 * DH), BF16),
            resident((groups, DH, DH)),
        ),
        in_specs=[HBM] * 3,
        out_specs=(VMEM,) * 4,
        scratch_shapes=[
            pltpu.SMEM((batch_count,), jnp.int32),
            pltpu.VMEM((groups, tokens, DH), F32),
            pltpu.VMEM((groups, tokens, DH), F32),
            pltpu.SemaphoreType.DMA(()),
            pltpu.SemaphoreType.DMA((2, groups, tokens // LOAD)),
        ],
        name="state",
    )(*map(leave, (span_length.reshape(batch_count), keys, values)))
    state, queries, cotangents, gains, selectors, level_table = lax.optimization_barrier(
        (state, queries, cotangents, gains, selectors, level_table)
    )

    weights, scaled = call(
        functools.partial(token_kernel, heads),
        out_shape=(
            resident((level_count + 1, groups, tokens // LANES, LANES)),
            resident((groups, DH, tokens)),
        ),
        in_specs=[SMEM] + [VMEM] * 3,
        out_specs=(VMEM,) * 2,
        name="token",
    )(level_table.T, selectors, cotangents, gains)

    buckets = []
    pending = state
    for level in range(level_count):
        buckets.append(partner(pending, "seq", level))
        pending = pending + buckets[-1]

    weighted_high, weighted_low, local_sum = call(
        local_kernel,
        out_shape=(
            resident((groups, stacked, tokens), BF16),
            resident((groups, stacked, tokens), BF16),
            resident((groups, DH, tokens)),
        ),
        in_specs=[VMEM] * 5,
        out_specs=(VMEM,) * 3,
        scratch_shapes=[pltpu.VMEM((2, DH, CHUNK), BF16)] * 2,
        name="local",
    )(*map(keep, (weights, queries, key_parts, value_parts, prefixes)))

    combined, sums = call(
        functools.partial(combine_kernel, heads),
        out_shape=(
            resident((groups, DH, tokens)),
            resident((2, batch_count, tokens // LANES, LANES)),
        ),
        in_specs=[VMEM] * (4 + level_count),
        out_specs=(VMEM,) * 2,
        name="combine",
    )(*map(keep, (local_sum, weighted_high, weighted_low, scaled, *buckets)))

    head_bits = lax.axis_size("head").bit_length() - 1
    rounds = [(1, 3, 2)[: (1 << min(2, head_bits)) - 1]]
    rounds += [(1 << level,) for level in range(2, head_bits)]
    for masks in rounds:
        sums = exchange(sums, "head", masks)

    top_grad, grad_parts = call(
        functools.partial(top_gradient_kernel, heads, full_width),
        out_shape=(resident((groups, DH, DH)), resident((groups, 2 * DH, tokens), BF16)),
        in_specs=[VMEM] * 5,
        out_specs=(VMEM,) * 2,
        name="top_gradient",
    )(*map(keep, (sums, combined, scaled, weighted_high, weighted_low)))
    grads = call(
        rest_gradient_kernel,
        out_shape=(resident((groups, DH, DH)),) * (level_count - 1),
        in_specs=[VMEM] * 3,
        out_specs=(VMEM,) * (level_count - 1),
        name="rest_gradient",
    )(*map(keep, (grad_parts, weighted_high, weighted_low)))

    attended = call(
        functools.partial(attended_kernel, heads, full_width),
        out_shape=jax.ShapeDtypeStruct((groups, tokens, DH), F32),
        in_specs=[VMEM] * 3,
        out_specs=HBM,
        scratch_shapes=[
            pltpu.VMEM((groups, tokens, DH), F32),
            pltpu.SemaphoreType.DMA((groups, tokens // LOAD)),
        ],
        name="attended",
    )(keep(sums), keep(combined), gains)

    total = partner(top_grad, "seq", level_count - 1)
    parts = []
    for level in reversed(range(level_count - 1)):
        total = sum(parts, total)
        received = partner(grads[level], "seq", level)
        parts = [partner(total, "seq", level), received]
    total = call(
        finish_kernel,
        out_shape=jax.ShapeDtypeStruct((groups, DH, DH), F32),
        in_specs=[VMEM] * 3,
        out_specs=VMEM,
        name="finish",
    )(*map(keep, (total, *parts)))

    def merge(rows, count):
        rows = rows.reshape(batch_count, heads, count, DH)
        return rows.transpose(0, 2, 1, 3).reshape(batch_count, count, heads * DH)

    return merge(attended, tokens), merge(total, DH)[:, None]


def solution(mesh):
    return jax.shard_map(
        body,
        mesh=mesh,
        in_specs=(
            P(None, "seq", "head"),
            P(None, "seq", "head"),
            P(None, "seq", "head"),
            P(None, "seq", "head"),
            P(None, "head", "seq"),
            P(),
            P(None, "seq"),
            P("head"),
        ),
        out_specs=(P(None, "seq", "head"), P(None, "seq", None, "head")),
        check_vma=False,
    )
```

```python
import functools

import jax
import jax.numpy as jnp
from jax import lax
from jax.experimental import pallas as pl
from jax.experimental.pallas import tpu as pltpu
from jax.sharding import PartitionSpec as P

DH = 128
LANES = 128
CHUNK = 256
LOAD = 1024
EPSILON = 1e-06
GRANT = 8 << 20
F32, BF16 = jnp.float32, jnp.bfloat16
NN = (((1,), (0,)), ((), ()))
NT = (((1,), (1,)), ((), ()))
VMEM = pl.BlockSpec(memory_space=pltpu.VMEM)
SMEM = pl.BlockSpec(memory_space=pltpu.SMEM)
HBM = pl.BlockSpec(memory_space=pl.ANY)


def dot(left, right, dims=NN):
    return lax.dot_general(left, right, dims, preferred_element_type=F32)


def halves(array):
    high = array.astype(BF16)
    return high, (array - high.astype(F32)).astype(BF16)


def chunk_states(groups, tokens, spans, key_at, value_at, outs, ready=None):
    key_out, value_out, prefix_out, state_out = outs
    spots = [(group, chunk) for group in range(groups) for chunk in range(tokens // CHUNK)]

    def prepare(group, chunk):
        if ready is not None:
            ready(group, chunk)
        rows = pl.ds(chunk * CHUNK, CHUNK)
        live = key_at(group, rows)
        if (chunk + 1) * CHUNK > tokens // 2:
            position = lax.broadcasted_iota(jnp.int32, (CHUNK, DH), 0)
            live = jnp.where(position < spans[group] - chunk * CHUNK, live, 0.0)
        key_out[group, rows, :] = jnp.concatenate(halves(live), axis=1)
        value_out[group, :, rows] = jnp.concatenate(halves(value_at(group, rows).T), axis=0)

    prepare(*spots[0])
    total = None
    for index, (group, chunk) in enumerate(spots):
        if index + 1 < len(spots):
            prepare(*spots[index + 1])
        rows = pl.ds(chunk * CHUNK, CHUNK)
        total = jnp.zeros((DH, DH), F32) if chunk == 0 else total
        prefix_out[group, chunk] = total
        square = dot(value_out[group, :, rows], key_out[group, rows, :])
        square = square[:DH] + square[DH:]
        total = total + (square[:, :DH] + square[:, DH:])
        if chunk == tokens // CHUNK - 1:
            state_out[group] = total


def level_weights(table_ref, selector_ref, weight_out):
    levels, choices = table_ref.shape
    for group in range(selector_ref.shape[0]):
        selector = selector_ref[group]
        for level in range(levels):
            weight = jnp.zeros(selector.shape, F32)
            for choice in range(choices):
                weight = jnp.where(selector == choice, table_ref[level, choice], weight)
            weight_out[level, group] = weight


def state_kernel(heads, span_hbm, table_hbm, selector_hbm, key_hbm, value_hbm, *refs):
    *outs, weight_out = refs[:5]
    span_ref, table_ref, selector_ref, key_ref, value_ref, small_sems, sems = refs[5:]
    groups, tokens, _ = key_ref.shape
    small = [
        pltpu.make_async_copy(source, target, small_sems.at[index])
        for index, (source, target) in enumerate(
            ((span_hbm, span_ref), (table_hbm, table_ref), (selector_hbm, selector_ref))
        )
    ]
    for copy in small:
        copy.start()
    loads = {}
    for group in range(groups):
        for load in range(tokens // LOAD):
            rows = pl.ds(load * LOAD, LOAD)
            loads[group, load] = [
                pltpu.make_async_copy(
                    source.at[group, rows], target.at[group, rows], sems.at[kind, group, load]
                )
                for kind, (source, target) in enumerate(
                    ((key_hbm, key_ref), (value_hbm, value_ref))
                )
            ]
            for copy in loads[group, load]:
                copy.start()
    small[0].wait()

    def ready(group, chunk):
        if chunk * CHUNK % LOAD == 0:
            for copy in loads[group, chunk * CHUNK // LOAD]:
                copy.wait()
        if group == 0 and (chunk + 1) * CHUNK == tokens:
            for copy in small[1:]:
                copy.wait()
            level_weights(table_ref, selector_ref, weight_out)

    chunk_states(
        groups,
        tokens,
        [span_ref[group // heads] for group in range(groups)],
        lambda group, rows: key_ref[group, rows, :],
        lambda group, rows: value_ref[group, rows, :],
        outs,
        ready,
    )


def causal_halves(scores, ahead):
    strips = []
    for row in range(0, CHUNK, LANES):
        blocks = []
        for column in range(0, CHUNK, LANES):
            block = scores[row : row + LANES, column : column + LANES]
            if row == column:
                block = jnp.where(ahead, block, 0.0)
            zero = jnp.zeros(block.shape, BF16)
            blocks.append((zero, zero) if row > column else halves(block))
        strips.append([jnp.concatenate(parts, axis=1) for parts in zip(*blocks)])
    return [jnp.concatenate(parts, axis=0) for parts in zip(*strips)]


def scale_kernel(heads, cotangent_ref, gain_ref, scaled_out):
    groups, tokens, _ = cotangent_ref.shape
    for group in range(groups):
        gain = gain_ref[pl.ds(group % heads, 1), :]
        for chunk in range(tokens // CHUNK):
            rows = pl.ds(chunk * CHUNK, CHUNK)
            scaled_out[group, :, rows] = (cotangent_ref[group, rows, :] * gain).T


def local_kernel(weight_ref, query_ref, key_ref, value_ref, prefix_ref, *refs):
    high_out, low_out, local_out, high_own, low_own = refs
    groups, tokens, _ = query_ref.shape
    levels = weight_ref.shape[0]
    ahead = lax.broadcasted_iota(jnp.int32, (LANES, LANES), 0) <= lax.broadcasted_iota(
        jnp.int32, (LANES, LANES), 1
    )
    spots = [(group, chunk) for group in range(groups) for chunk in range(tokens // CHUNK)]

    def prepare(index):
        group, chunk = spots[index]
        rows = pl.ds(chunk * CHUNK, CHUNK)
        query = query_ref[group, rows, :].T
        high_own[index % 2], low_own[index % 2] = halves(
            query * token_row(weight_ref.at[0, group], chunk)
        )
        for level in range(1, levels):
            high, low = halves(query * token_row(weight_ref.at[level, group], chunk))
            high_out[group, pl.ds((level - 1) * DH, DH), rows] = high
            low_out[group, pl.ds((level - 1) * DH, DH), rows] = low

    prepare(0)
    for index, (group, chunk) in enumerate(spots):
        if index + 1 < len(spots):
            prepare(index + 1)
        rows = pl.ds(chunk * CHUNK, CHUNK)
        high, low = high_own[index % 2], low_own[index % 2]
        prefix = jnp.concatenate(halves(prefix_ref[group, chunk]), axis=1)
        left = jnp.concatenate([key_ref[group, rows, :], prefix], axis=0)
        mixed = dot(left, jnp.concatenate([high, high], axis=0)) + dot(left[:, :DH], low)
        scores_high, scores_low = causal_halves(mixed[:CHUNK], ahead)
        values = value_ref[group, :, rows]
        near = dot(values, scores_high)
        near = near[:DH] + near[DH:] + dot(values[:DH], scores_low)
        local_out[group, :, rows] = near + mixed[CHUNK:]


def combine_kernel(
    heads, local_ref, high_ref, low_ref, scaled_ref, *refs
):
    *bucket_refs, combined_out, sums_out = refs
    groups, _, tokens = local_ref.shape
    seq_index = lax.axis_index("seq")
    per = CHUNK // LANES
    for group in range(groups):
        buckets = []
        for level, bucket_ref in enumerate(bucket_refs):
            reads = seq_index >> level & 1
            buckets.append(jnp.where(reads == 1, bucket_ref[group], 0.0))
        bucket_high, bucket_low = halves(jnp.concatenate(buckets, axis=1))
        both = jnp.concatenate([bucket_high, bucket_low], axis=0)
        for chunk in range(tokens // CHUNK):
            rows = pl.ds(chunk * CHUNK, CHUNK)
            square = dot(both, high_ref[group, :, rows])
            square = square[:DH] + square[DH:] + dot(bucket_high, low_ref[group, :, rows])
            combined = square + local_ref[group, :, rows]
            combined_out[group, :, rows] = combined
            sums = (
                jnp.sum(combined * combined, axis=0, keepdims=True),
                jnp.sum(combined * scaled_ref[group, :, rows], axis=0, keepdims=True),
            )
            for kind in range(2):
                for part in range(per):
                    spot = (kind, group // heads, pl.ds(chunk * per + part, 1))
                    row = sums[kind][:, part * LANES : (part + 1) * LANES]
                    sums_out[spot] = row if group % heads == 0 else sums_out[spot] + row


def factors(sums_ref, batch, full_width):
    inverse = lax.rsqrt(sums_ref[0, batch] / full_width + EPSILON)
    return inverse, inverse * inverse * inverse * sums_ref[1, batch] / full_width


def token_row(array, chunk):
    per = CHUNK // LANES
    spots = range(chunk * per, (chunk + 1) * per)
    return jnp.concatenate([array[spot : spot + 1, :] for spot in spots], axis=1)


def fold(total):
    total = total[:DH] + total[DH:]
    return (total[:, :DH] + total[:, DH:]).T


def top_gradient_kernel(
    heads, full_width, sums_ref, combined_ref, scaled_ref, high_ref, low_ref, *outs
):
    grad_out, parts_out = outs
    groups, _, tokens = combined_ref.shape
    level = high_ref.shape[1] // DH - 1
    top = pl.ds(level * DH, DH)
    reads = lax.axis_index("seq") >> level & 1
    for group in range(groups):
        inverse, pull = factors(sums_ref, group // heads, full_width)
        for chunk in range(tokens // CHUNK):
            rows = pl.ds(chunk * CHUNK, CHUNK)
            grad = scaled_ref[group, :, rows] * token_row(inverse, chunk) - combined_ref[
                group, :, rows
            ] * token_row(pull, chunk)
            parts_out[group, :, rows] = jnp.concatenate(halves(grad), axis=0)
        weighted = jnp.concatenate([high_ref[group, top, :], low_ref[group, top, :]], 0)
        total = dot(parts_out[group], weighted, NT)
        grad_out[group] = jnp.where(reads == 1, fold(total), 0.0)


def rest_gradient_kernel(parts_ref, high_ref, low_ref, *grad_outs):
    groups, _, _ = parts_ref.shape
    for level, grad_out in enumerate(grad_outs):
        spot = pl.ds(level * DH, DH)
        reads = lax.axis_index("seq") >> level & 1
        for group in range(groups):
            weighted = jnp.concatenate([high_ref[group, spot, :], low_ref[group, spot, :]], 0)
            total = dot(parts_ref[group], weighted, NT)
            grad_out[group] = jnp.where(reads == 1, fold(total), 0.0)


def finish_kernel(*refs):
    *part_refs, out_ref = refs
    total = part_refs[0][...]
    for part_ref in part_refs[1:]:
        total = total + part_ref[...]
    out_ref[...] = total


def attended_kernel(
    heads, full_width, sums_ref, combined_ref, gain_ref, attended_hbm, attended_ref, sems
):
    groups, _, tokens = combined_ref.shape
    copies = []
    for group in range(groups):
        gain = gain_ref[pl.ds(group % heads, 1), :]
        inverse, _ = factors(sums_ref, group // heads, full_width)
        for chunk in range(tokens // CHUNK):
            rows = pl.ds(chunk * CHUNK, CHUNK)
            scaled = combined_ref[group, :, rows] * token_row(inverse, chunk)
            attended_ref[group, rows, :] = scaled.T * gain
            if (chunk + 1) * CHUNK % LOAD == 0:
                load = (chunk + 1) * CHUNK // LOAD - 1
                rows = pl.ds(load * LOAD, LOAD)
                copies.append(
                    pltpu.make_async_copy(
                        attended_ref.at[group, rows],
                        attended_hbm.at[group, rows],
                        sems.at[group, load],
                    )
                )
                copies[-1].start()
    for copy in copies:
        copy.wait()


def resident(shape, dtype=F32):
    return pltpu.VMEM(shape, dtype)


def keep(array):
    return pltpu.with_memory_space_constraint(array, pltpu.VMEM)


def leave(array):
    return pltpu.with_memory_space_constraint(array, pltpu.HBM)


def partner(shard, axis, stride):
    return lax.ppermute(shard, axis, [(i, i ^ 1 << stride) for i in range(lax.axis_size(axis))])


def exchange(shard, axis, masks):
    size = lax.axis_size(axis)
    others = [lax.ppermute(shard, axis, [(i, i ^ mask) for i in range(size)]) for mask in masks]
    return sum(others, shard)


def body(
    query_rows, key_rows, value_rows, cotangent, selector, level_table, span_length, norm_gain
):
    batch_count, tokens, local_width = query_rows.shape
    heads = local_width // DH
    groups = batch_count * heads
    full_width = local_width * lax.axis_size("head")
    level_count = lax.axis_size("seq").bit_length() - 1

    def split(rows):
        rows = rows.reshape(batch_count, tokens, heads, DH)
        return rows.transpose(0, 2, 1, 3).reshape(groups, tokens, DH)

    queries, keys, values, cotangents = map(split, (query_rows, key_rows, value_rows, cotangent))
    selectors = selector.reshape(groups, tokens // LANES, LANES)
    gains = norm_gain.reshape(heads, DH)
    chunks = tokens // CHUNK
    stacked = level_count * DH
    call = functools.partial(
        pl.pallas_call, compiler_params=pltpu.CompilerParams(vmem_limit_bytes=GRANT)
    )

    key_parts, value_parts, prefixes, state, weights = call(
        functools.partial(state_kernel, heads),
        out_shape=(
            resident((groups, tokens, 2 * DH), BF16),
            resident((groups, 2 * DH, tokens), BF16),
            resident((groups, chunks, DH, DH)),
            resident((groups, DH, DH)),
            resident((level_count + 1, groups, tokens // LANES, LANES)),
        ),
        in_specs=[HBM] * 5,
        out_specs=(VMEM,) * 5,
        scratch_shapes=[
            pltpu.SMEM((batch_count,), jnp.int32),
            pltpu.SMEM(level_table.shape[::-1], F32),
            pltpu.VMEM(selectors.shape, jnp.int32),
            pltpu.VMEM((groups, tokens, DH), F32),
            pltpu.VMEM((groups, tokens, DH), F32),
            pltpu.SemaphoreType.DMA((3,)),
            pltpu.SemaphoreType.DMA((2, groups, tokens // LOAD)),
        ],
        name="state",
    )(
        *map(
            leave,
            (span_length.reshape(batch_count), level_table.T, selectors, keys, values),
        )
    )
    state, queries, cotangents, gains = lax.optimization_barrier(
        (state, queries, cotangents, gains)
    )

    buckets = []
    for level in reversed(range(level_count)):
        bucket = partner(state, "seq", level)
        for lower in reversed(range(level)):
            bucket = bucket + partner(bucket, "seq", lower)
        buckets.insert(0, bucket)

    weighted_high, weighted_low, local_sum = call(
        local_kernel,
        out_shape=(
            resident((groups, stacked, tokens), BF16),
            resident((groups, stacked, tokens), BF16),
            resident((groups, DH, tokens)),
        ),
        in_specs=[VMEM] * 5,
        out_specs=(VMEM,) * 3,
        scratch_shapes=[pltpu.VMEM((2, DH, CHUNK), BF16)] * 2,
        name="local",
    )(*map(keep, (weights, queries, key_parts, value_parts, prefixes)))

    scaled = call(
        functools.partial(scale_kernel, heads),
        out_shape=resident((groups, DH, tokens)),
        in_specs=[VMEM] * 2,
        out_specs=VMEM,
        name="scale",
    )(cotangents, gains)

    combined, sums = call(
        functools.partial(combine_kernel, heads),
        out_shape=(
            resident((groups, DH, tokens)),
            resident((2, batch_count, tokens // LANES, LANES)),
        ),
        in_specs=[VMEM] * (4 + level_count),
        out_specs=(VMEM,) * 2,
        name="combine",
    )(*map(keep, (local_sum, weighted_high, weighted_low, scaled, *buckets)))

    head_bits = lax.axis_size("head").bit_length() - 1
    rounds = [(1, 3, 2)[: (1 << min(2, head_bits)) - 1]]
    rounds += [(1 << level,) for level in range(2, head_bits)]
    for masks in rounds:
        sums = exchange(sums, "head", masks)

    top_grad, grad_parts = call(
        functools.partial(top_gradient_kernel, heads, full_width),
        out_shape=(resident((groups, DH, DH)), resident((groups, 2 * DH, tokens), BF16)),
        in_specs=[VMEM] * 5,
        out_specs=(VMEM,) * 2,
        name="top_gradient",
    )(*map(keep, (sums, combined, scaled, weighted_high, weighted_low)))
    grads = call(
        rest_gradient_kernel,
        out_shape=(resident((groups, DH, DH)),) * (level_count - 1),
        in_specs=[VMEM] * 3,
        out_specs=(VMEM,) * (level_count - 1),
        name="rest_gradient",
    )(*map(keep, (grad_parts, weighted_high, weighted_low)))

    attended = call(
        functools.partial(attended_kernel, heads, full_width),
        out_shape=jax.ShapeDtypeStruct((groups, tokens, DH), F32),
        in_specs=[VMEM] * 3,
        out_specs=HBM,
        scratch_shapes=[
            pltpu.VMEM((groups, tokens, DH), F32),
            pltpu.SemaphoreType.DMA((groups, tokens // LOAD)),
        ],
        name="attended",
    )(keep(sums), keep(combined), gains)

    total = partner(top_grad, "seq", level_count - 1)
    parts = []
    for level in reversed(range(level_count - 1)):
        total = sum(parts, total)
        received = partner(grads[level], "seq", level)
        parts = [partner(total, "seq", level), received]
    total = call(
        finish_kernel,
        out_shape=jax.ShapeDtypeStruct((groups, DH, DH), F32),
        in_specs=[VMEM] * 3,
        out_specs=VMEM,
        name="finish",
    )(*map(keep, (total, *parts)))

    def merge(rows, count):
        rows = rows.reshape(batch_count, heads, count, DH)
        return rows.transpose(0, 2, 1, 3).reshape(batch_count, count, heads * DH)

    return merge(attended, tokens), merge(total, DH)[:, None]


def solution(mesh):
    return jax.shard_map(
        body,
        mesh=mesh,
        in_specs=(
            P(None, "seq", "head"),
            P(None, "seq", "head"),
            P(None, "seq", "head"),
            P(None, "seq", "head"),
            P(None, "head", "seq"),
            P(),
            P(None, "seq"),
            P("head"),
        ),
        out_specs=(P(None, "seq", "head"), P(None, "seq", None, "head")),
        check_vma=False,
    )
```

```python
import functools

import jax
import jax.numpy as jnp
from jax import lax
from jax.experimental import pallas as pl
from jax.experimental.pallas import tpu as pltpu
from jax.sharding import PartitionSpec as P

DH = 128
LANES = 128
CHUNK = 256
LOAD = 1024
EPSILON = 1e-06
GRANT = 8 << 20
F32, BF16 = jnp.float32, jnp.bfloat16
NN = (((1,), (0,)), ((), ()))
NT = (((1,), (1,)), ((), ()))
VMEM = pl.BlockSpec(memory_space=pltpu.VMEM)
SMEM = pl.BlockSpec(memory_space=pltpu.SMEM)
HBM = pl.BlockSpec(memory_space=pl.ANY)


def dot(left, right, dims=NN):
    return lax.dot_general(left, right, dims, preferred_element_type=F32)


def halves(array):
    high = array.astype(BF16)
    return high, (array - high.astype(F32)).astype(BF16)


def chunk_states(groups, tokens, span_at, key_at, value_at, outs, ready):
    key_out, value_out, prefix_out, state_out = outs
    spots = [(group, chunk) for group in range(groups) for chunk in range(tokens // CHUNK)]

    def prepare(group, chunk):
        ready(group, chunk)
        rows = pl.ds(chunk * CHUNK, CHUNK)
        live = key_at(group, rows)
        if (chunk + 1) * CHUNK > tokens // 2:
            position = lax.broadcasted_iota(jnp.int32, (CHUNK, DH), 0)
            live = jnp.where(position < span_at(group) - chunk * CHUNK, live, 0.0)
        key_out[group, rows, :] = jnp.concatenate(halves(live), axis=1)
        value_out[group, :, rows] = jnp.concatenate(halves(value_at(group, rows).T), axis=0)

    prepare(*spots[0])
    total = None
    for index, (group, chunk) in enumerate(spots):
        if index + 1 < len(spots):
            prepare(*spots[index + 1])
        rows = pl.ds(chunk * CHUNK, CHUNK)
        total = jnp.zeros((DH, DH), F32) if chunk == 0 else total
        prefix_out[group, chunk] = total
        square = dot(value_out[group, :, rows], key_out[group, rows, :])
        square = square[:DH] + square[DH:]
        total = total + (square[:, :DH] + square[:, DH:])
        if chunk == tokens // CHUNK - 1:
            state_out[group] = total


def level_weights(table_ref, selector_ref, weight_out):
    levels, choices = table_ref.shape
    for group in range(selector_ref.shape[0]):
        selector = selector_ref[group]
        for level in range(levels):
            weight = jnp.zeros(selector.shape, F32)
            for choice in range(choices):
                weight = jnp.where(selector == choice, table_ref[level, choice], weight)
            weight_out[level, group] = weight


def state_kernel(heads, span_hbm, table_hbm, selector_hbm, key_hbm, value_hbm, *refs):
    *outs, weight_out = refs[:5]
    span_ref, table_ref, selector_ref, key_ref, value_ref, small_sems, sems = refs[5:]
    groups, tokens, _ = key_ref.shape
    small = [
        pltpu.make_async_copy(source, target, small_sems.at[index])
        for index, (source, target) in enumerate(
            ((span_hbm, span_ref), (table_hbm, table_ref), (selector_hbm, selector_ref))
        )
    ]
    for copy in small:
        copy.start()
    loads = {}
    for group in range(groups):
        for load in range(tokens // LOAD):
            rows = pl.ds(load * LOAD, LOAD)
            loads[group, load] = [
                pltpu.make_async_copy(
                    source.at[group, rows], target.at[group, rows], sems.at[kind, group, load]
                )
                for kind, (source, target) in enumerate(
                    ((key_hbm, key_ref), (value_hbm, value_ref))
                )
            ]
            for copy in loads[group, load]:
                copy.start()

    def ready(group, chunk):
        if chunk * CHUNK % LOAD == 0:
            for copy in loads[group, chunk * CHUNK // LOAD]:
                copy.wait()
        if group == 0 and chunk == tokens // 2 // CHUNK:
            small[0].wait()
        if group == groups // 2 and chunk == 0:
            for copy in small[1:]:
                copy.wait()
            level_weights(table_ref, selector_ref, weight_out)

    chunk_states(
        groups,
        tokens,
        lambda group: span_ref[group // heads],
        lambda group, rows: key_ref[group, rows, :],
        lambda group, rows: value_ref[group, rows, :],
        outs,
        ready,
    )


def causal_halves(scores, ahead):
    strips = []
    for row in range(0, CHUNK, LANES):
        blocks = []
        for column in range(0, CHUNK, LANES):
            block = scores[row : row + LANES, column : column + LANES]
            if row == column:
                block = jnp.where(ahead, block, 0.0)
            zero = jnp.zeros(block.shape, BF16)
            blocks.append((zero, zero) if row > column else halves(block))
        strips.append([jnp.concatenate(parts, axis=1) for parts in zip(*blocks)])
    return [jnp.concatenate(parts, axis=0) for parts in zip(*strips)]


def scale_kernel(heads, cotangent_ref, gain_ref, scaled_out):
    groups, tokens, _ = cotangent_ref.shape
    for group in range(groups):
        gain = gain_ref[pl.ds(group % heads, 1), :]
        for chunk in range(tokens // CHUNK):
            rows = pl.ds(chunk * CHUNK, CHUNK)
            scaled_out[group, :, rows] = (cotangent_ref[group, rows, :] * gain).T


def local_kernel(weight_ref, query_ref, key_ref, value_ref, prefix_ref, *refs):
    high_out, low_out, local_out, high_own, low_own = refs
    groups, tokens, _ = query_ref.shape
    levels = weight_ref.shape[0]
    ahead = lax.broadcasted_iota(jnp.int32, (LANES, LANES), 0) <= lax.broadcasted_iota(
        jnp.int32, (LANES, LANES), 1
    )
    spots = [(group, chunk) for group in range(groups) for chunk in range(tokens // CHUNK)]

    def prepare(index):
        group, chunk = spots[index]
        rows = pl.ds(chunk * CHUNK, CHUNK)
        query = query_ref[group, rows, :].T
        high_own[index % 2], low_own[index % 2] = halves(
            query * token_row(weight_ref.at[0, group], chunk)
        )
        for level in range(1, levels):
            high, low = halves(query * token_row(weight_ref.at[level, group], chunk))
            high_out[group, pl.ds((level - 1) * DH, DH), rows] = high
            low_out[group, pl.ds((level - 1) * DH, DH), rows] = low

    prepare(0)
    for index, (group, chunk) in enumerate(spots):
        if index + 1 < len(spots):
            prepare(index + 1)
        rows = pl.ds(chunk * CHUNK, CHUNK)
        high, low = high_own[index % 2], low_own[index % 2]
        prefix = jnp.concatenate(halves(prefix_ref[group, chunk]), axis=1)
        left = jnp.concatenate([key_ref[group, rows, :], prefix], axis=0)
        mixed = dot(left, jnp.concatenate([high, high], axis=0)) + dot(left[:, :DH], low)
        scores_high, scores_low = causal_halves(mixed[:CHUNK], ahead)
        values = value_ref[group, :, rows]
        near = dot(values, scores_high)
        near = near[:DH] + near[DH:] + dot(values[:DH], scores_low)
        local_out[group, :, rows] = near + mixed[CHUNK:]


def combine_kernel(
    heads, local_ref, high_ref, low_ref, scaled_ref, *refs
):
    *bucket_refs, combined_out, sums_out = refs
    groups, _, tokens = local_ref.shape
    seq_index = lax.axis_index("seq")
    per = CHUNK // LANES
    for group in range(groups):
        buckets = []
        for level, bucket_ref in enumerate(bucket_refs):
            reads = seq_index >> level & 1
            buckets.append(jnp.where(reads == 1, bucket_ref[group], 0.0))
        bucket_high, bucket_low = halves(jnp.concatenate(buckets, axis=1))
        both = jnp.concatenate([bucket_high, bucket_low], axis=0)
        for chunk in range(tokens // CHUNK):
            rows = pl.ds(chunk * CHUNK, CHUNK)
            square = dot(both, high_ref[group, :, rows])
            square = square[:DH] + square[DH:] + dot(bucket_high, low_ref[group, :, rows])
            combined = square + local_ref[group, :, rows]
            combined_out[group, :, rows] = combined
            sums = (
                jnp.sum(combined * combined, axis=0, keepdims=True),
                jnp.sum(combined * scaled_ref[group, :, rows], axis=0, keepdims=True),
            )
            for kind in range(2):
                for part in range(per):
                    spot = (kind, group // heads, pl.ds(chunk * per + part, 1))
                    row = sums[kind][:, part * LANES : (part + 1) * LANES]
                    sums_out[spot] = row if group % heads == 0 else sums_out[spot] + row


def factors(sums_ref, batch, full_width):
    inverse = lax.rsqrt(sums_ref[0, batch] / full_width + EPSILON)
    return inverse, inverse * inverse * inverse * sums_ref[1, batch] / full_width


def token_row(array, chunk):
    per = CHUNK // LANES
    spots = range(chunk * per, (chunk + 1) * per)
    return jnp.concatenate([array[spot : spot + 1, :] for spot in spots], axis=1)


def fold(total):
    total = total[:DH] + total[DH:]
    return (total[:, :DH] + total[:, DH:]).T


def top_gradient_kernel(
    heads, full_width, sums_ref, combined_ref, scaled_ref, high_ref, low_ref, *outs
):
    grad_out, parts_out = outs
    groups, _, tokens = combined_ref.shape
    level = high_ref.shape[1] // DH - 1
    top = pl.ds(level * DH, DH)
    reads = lax.axis_index("seq") >> level & 1
    for group in range(groups):
        inverse, pull = factors(sums_ref, group // heads, full_width)
        for chunk in range(tokens // CHUNK):
            rows = pl.ds(chunk * CHUNK, CHUNK)
            grad = scaled_ref[group, :, rows] * token_row(inverse, chunk) - combined_ref[
                group, :, rows
            ] * token_row(pull, chunk)
            parts_out[group, :, rows] = jnp.concatenate(halves(grad), axis=0)
        weighted = jnp.concatenate([high_ref[group, top, :], low_ref[group, top, :]], 0)
        total = dot(parts_out[group], weighted, NT)
        grad_out[group] = jnp.where(reads == 1, fold(total), 0.0)


def rest_gradient_kernel(parts_ref, high_ref, low_ref, *grad_outs):
    groups, _, _ = parts_ref.shape
    for level, grad_out in enumerate(grad_outs):
        spot = pl.ds(level * DH, DH)
        reads = lax.axis_index("seq") >> level & 1
        for group in range(groups):
            weighted = jnp.concatenate([high_ref[group, spot, :], low_ref[group, spot, :]], 0)
            total = dot(parts_ref[group], weighted, NT)
            grad_out[group] = jnp.where(reads == 1, fold(total), 0.0)


def finish_kernel(*refs):
    *part_refs, out_ref = refs
    total = part_refs[0][...]
    for part_ref in part_refs[1:]:
        total = total + part_ref[...]
    out_ref[...] = total


def attended_kernel(
    heads, full_width, sums_ref, combined_ref, gain_ref, attended_hbm, attended_ref, sems
):
    groups, _, tokens = combined_ref.shape
    copies = []
    for group in range(groups):
        gain = gain_ref[pl.ds(group % heads, 1), :]
        inverse, _ = factors(sums_ref, group // heads, full_width)
        for chunk in range(tokens // CHUNK):
            rows = pl.ds(chunk * CHUNK, CHUNK)
            scaled = combined_ref[group, :, rows] * token_row(inverse, chunk)
            attended_ref[group, rows, :] = scaled.T * gain
            if (chunk + 1) * CHUNK % LOAD == 0:
                load = (chunk + 1) * CHUNK // LOAD - 1
                rows = pl.ds(load * LOAD, LOAD)
                copies.append(
                    pltpu.make_async_copy(
                        attended_ref.at[group, rows],
                        attended_hbm.at[group, rows],
                        sems.at[group, load],
                    )
                )
                copies[-1].start()
    for copy in copies:
        copy.wait()


def resident(shape, dtype=F32):
    return pltpu.VMEM(shape, dtype)


def keep(array):
    return pltpu.with_memory_space_constraint(array, pltpu.VMEM)


def leave(array):
    return pltpu.with_memory_space_constraint(array, pltpu.HBM)


def partner(shard, axis, stride):
    return lax.ppermute(shard, axis, [(i, i ^ 1 << stride) for i in range(lax.axis_size(axis))])


def exchange(shard, axis, masks):
    size = lax.axis_size(axis)
    others = [lax.ppermute(shard, axis, [(i, i ^ mask) for i in range(size)]) for mask in masks]
    return sum(others, shard)


def body(
    query_rows, key_rows, value_rows, cotangent, selector, level_table, span_length, norm_gain
):
    batch_count, tokens, local_width = query_rows.shape
    heads = local_width // DH
    groups = batch_count * heads
    full_width = local_width * lax.axis_size("head")
    level_count = lax.axis_size("seq").bit_length() - 1

    def split(rows):
        rows = rows.reshape(batch_count, tokens, heads, DH)
        return rows.transpose(0, 2, 1, 3).reshape(groups, tokens, DH)

    queries, keys, values, cotangents = map(split, (query_rows, key_rows, value_rows, cotangent))
    selectors = selector.reshape(groups, tokens // LANES, LANES)
    gains = norm_gain.reshape(heads, DH)
    chunks = tokens // CHUNK
    stacked = level_count * DH
    call = functools.partial(
        pl.pallas_call, compiler_params=pltpu.CompilerParams(vmem_limit_bytes=GRANT)
    )

    key_parts, value_parts, prefixes, state, weights = call(
        functools.partial(state_kernel, heads),
        out_shape=(
            resident((groups, tokens, 2 * DH), BF16),
            resident((groups, 2 * DH, tokens), BF16),
            resident((groups, chunks, DH, DH)),
            resident((groups, DH, DH)),
            resident((level_count + 1, groups, tokens // LANES, LANES)),
        ),
        in_specs=[HBM] * 5,
        out_specs=(VMEM,) * 5,
        scratch_shapes=[
            pltpu.SMEM((batch_count,), jnp.int32),
            pltpu.SMEM(level_table.shape[::-1], F32),
            pltpu.VMEM(selectors.shape, jnp.int32),
            pltpu.VMEM((groups, tokens, DH), F32),
            pltpu.VMEM((groups, tokens, DH), F32),
            pltpu.SemaphoreType.DMA((3,)),
            pltpu.SemaphoreType.DMA((2, groups, tokens // LOAD)),
        ],
        name="state",
    )(
        *map(
            leave,
            (span_length.reshape(batch_count), level_table.T, selectors, keys, values),
        )
    )
    state, queries, cotangents, gains = lax.optimization_barrier(
        (state, queries, cotangents, gains)
    )

    buckets = []
    for level in reversed(range(level_count)):
        bucket = partner(state, "seq", level)
        for lower in reversed(range(level)):
            bucket = bucket + partner(bucket, "seq", lower)
        buckets.insert(0, bucket)

    weighted_high, weighted_low, local_sum = call(
        local_kernel,
        out_shape=(
            resident((groups, stacked, tokens), BF16),
            resident((groups, stacked, tokens), BF16),
            resident((groups, DH, tokens)),
        ),
        in_specs=[VMEM] * 5,
        out_specs=(VMEM,) * 3,
        scratch_shapes=[pltpu.VMEM((2, DH, CHUNK), BF16)] * 2,
        name="local",
    )(*map(keep, (weights, queries, key_parts, value_parts, prefixes)))

    scaled = call(
        functools.partial(scale_kernel, heads),
        out_shape=resident((groups, DH, tokens)),
        in_specs=[VMEM] * 2,
        out_specs=VMEM,
        name="scale",
    )(cotangents, gains)

    combined, sums = call(
        functools.partial(combine_kernel, heads),
        out_shape=(
            resident((groups, DH, tokens)),
            resident((2, batch_count, tokens // LANES, LANES)),
        ),
        in_specs=[VMEM] * (4 + level_count),
        out_specs=(VMEM,) * 2,
        name="combine",
    )(*map(keep, (local_sum, weighted_high, weighted_low, scaled, *buckets)))

    head_bits = lax.axis_size("head").bit_length() - 1
    rounds = [(1, 3, 2)[: (1 << min(2, head_bits)) - 1]]
    rounds += [(1 << level,) for level in range(2, head_bits)]
    for masks in rounds:
        sums = exchange(sums, "head", masks)

    top_grad, grad_parts = call(
        functools.partial(top_gradient_kernel, heads, full_width),
        out_shape=(resident((groups, DH, DH)), resident((groups, 2 * DH, tokens), BF16)),
        in_specs=[VMEM] * 5,
        out_specs=(VMEM,) * 2,
        name="top_gradient",
    )(*map(keep, (sums, combined, scaled, weighted_high, weighted_low)))
    grads = call(
        rest_gradient_kernel,
        out_shape=(resident((groups, DH, DH)),) * (level_count - 1),
        in_specs=[VMEM] * 3,
        out_specs=(VMEM,) * (level_count - 1),
        name="rest_gradient",
    )(*map(keep, (grad_parts, weighted_high, weighted_low)))

    attended = call(
        functools.partial(attended_kernel, heads, full_width),
        out_shape=jax.ShapeDtypeStruct((groups, tokens, DH), F32),
        in_specs=[VMEM] * 3,
        out_specs=HBM,
        scratch_shapes=[
            pltpu.VMEM((groups, tokens, DH), F32),
            pltpu.SemaphoreType.DMA((groups, tokens // LOAD)),
        ],
        name="attended",
    )(keep(sums), keep(combined), gains)

    total = partner(top_grad, "seq", level_count - 1)
    parts = []
    for level in reversed(range(level_count - 1)):
        total = sum(parts, total)
        received = partner(grads[level], "seq", level)
        parts = [partner(total, "seq", level), received]
    total = call(
        finish_kernel,
        out_shape=jax.ShapeDtypeStruct((groups, DH, DH), F32),
        in_specs=[VMEM] * 3,
        out_specs=VMEM,
        name="finish",
    )(*map(keep, (total, *parts)))

    def merge(rows, count):
        rows = rows.reshape(batch_count, heads, count, DH)
        return rows.transpose(0, 2, 1, 3).reshape(batch_count, count, heads * DH)

    return merge(attended, tokens), merge(total, DH)[:, None]


def solution(mesh):
    return jax.shard_map(
        body,
        mesh=mesh,
        in_specs=(
            P(None, "seq", "head"),
            P(None, "seq", "head"),
            P(None, "seq", "head"),
            P(None, "seq", "head"),
            P(None, "head", "seq"),
            P(),
            P(None, "seq"),
            P("head"),
        ),
        out_specs=(P(None, "seq", "head"), P(None, "seq", None, "head")),
        check_vma=False,
    )
```

```python
import functools

import jax
import jax.numpy as jnp
from jax import lax
from jax.experimental import pallas as pl
from jax.experimental.pallas import tpu as pltpu
from jax.sharding import PartitionSpec as P

DH = 128
LANES = 128
CHUNK = 256
LOAD = 2048
EPSILON = 1e-06
GRANT = 8 << 20
F32, BF16 = jnp.float32, jnp.bfloat16
NN = (((1,), (0,)), ((), ()))
NT = (((1,), (1,)), ((), ()))
VMEM = pl.BlockSpec(memory_space=pltpu.VMEM)
SMEM = pl.BlockSpec(memory_space=pltpu.SMEM)
HBM = pl.BlockSpec(memory_space=pl.ANY)


def dot(left, right, dims=NN):
    return lax.dot_general(left, right, dims, preferred_element_type=F32)


def halves(array):
    high = array.astype(BF16)
    return high, (array - high.astype(F32)).astype(BF16)


def chunk_states(groups, tokens, span_at, key_at, value_at, outs, ready):
    key_out, value_out, prefix_out, state_out = outs
    spots = [(group, chunk) for group in range(groups) for chunk in range(tokens // CHUNK)]

    def prepare(group, chunk):
        ready(group, chunk)
        rows = pl.ds(chunk * CHUNK, CHUNK)
        live = key_at(group, rows)
        if (chunk + 1) * CHUNK > tokens // 2:
            position = lax.broadcasted_iota(jnp.int32, (CHUNK, DH), 0)
            live = jnp.where(position < span_at(group) - chunk * CHUNK, live, 0.0)
        key_out[group, rows, :] = jnp.concatenate(halves(live), axis=1)
        value_out[group, :, rows] = jnp.concatenate(halves(value_at(group, rows).T), axis=0)

    prepare(*spots[0])
    total = None
    for index, (group, chunk) in enumerate(spots):
        if index + 1 < len(spots):
            prepare(*spots[index + 1])
        rows = pl.ds(chunk * CHUNK, CHUNK)
        total = jnp.zeros((DH, DH), F32) if chunk == 0 else total
        prefix_out[group, chunk] = total
        square = dot(value_out[group, :, rows], key_out[group, rows, :])
        square = square[:DH] + square[DH:]
        total = total + (square[:, :DH] + square[:, DH:])
        if chunk == tokens // CHUNK - 1:
            state_out[group] = total


def level_weights(table_ref, selector_ref, weight_out):
    levels, choices = table_ref.shape
    for group in range(selector_ref.shape[0]):
        selector = selector_ref[group]
        for level in range(levels):
            weight = jnp.zeros(selector.shape, F32)
            for choice in range(choices):
                weight = jnp.where(selector == choice, table_ref[level, choice], weight)
            weight_out[level, group] = weight


def state_kernel(heads, span_hbm, table_hbm, selector_hbm, key_hbm, value_hbm, *refs):
    *outs, weight_out = refs[:5]
    span_ref, table_ref, selector_ref, key_ref, value_ref, small_sems, sems = refs[5:]
    groups, tokens, _ = key_ref.shape
    small = [
        pltpu.make_async_copy(source, target, small_sems.at[index])
        for index, (source, target) in enumerate(
            ((span_hbm, span_ref), (table_hbm, table_ref), (selector_hbm, selector_ref))
        )
    ]
    for copy in small:
        copy.start()
    loads = {}
    for group in range(groups):
        for load in range(tokens // LOAD):
            rows = pl.ds(load * LOAD, LOAD)
            loads[group, load] = [
                pltpu.make_async_copy(
                    source.at[group, rows], target.at[group, rows], sems.at[kind, group, load]
                )
                for kind, (source, target) in enumerate(
                    ((key_hbm, key_ref), (value_hbm, value_ref))
                )
            ]
            for copy in loads[group, load]:
                copy.start()

    def ready(group, chunk):
        if chunk * CHUNK % LOAD == 0:
            for copy in loads[group, chunk * CHUNK // LOAD]:
                copy.wait()
        if group == 0 and chunk == tokens // 2 // CHUNK:
            small[0].wait()
        if group == groups // 2 and chunk == 0:
            for copy in small[1:]:
                copy.wait()
            level_weights(table_ref, selector_ref, weight_out)

    chunk_states(
        groups,
        tokens,
        lambda group: span_ref[group // heads],
        lambda group, rows: key_ref[group, rows, :],
        lambda group, rows: value_ref[group, rows, :],
        outs,
        ready,
    )


def causal_halves(scores, ahead):
    strips = []
    for row in range(0, CHUNK, LANES):
        blocks = []
        for column in range(0, CHUNK, LANES):
            block = scores[row : row + LANES, column : column + LANES]
            if row == column:
                block = jnp.where(ahead, block, 0.0)
            zero = jnp.zeros(block.shape, BF16)
            blocks.append((zero, zero) if row > column else halves(block))
        strips.append([jnp.concatenate(parts, axis=1) for parts in zip(*blocks)])
    return [jnp.concatenate(parts, axis=0) for parts in zip(*strips)]


def scale_kernel(heads, cotangent_ref, gain_ref, scaled_out):
    groups, tokens, _ = cotangent_ref.shape
    for group in range(groups):
        gain = gain_ref[pl.ds(group % heads, 1), :]
        for chunk in range(tokens // CHUNK):
            rows = pl.ds(chunk * CHUNK, CHUNK)
            scaled_out[group, :, rows] = (cotangent_ref[group, rows, :] * gain).T


def local_kernel(weight_ref, query_ref, key_ref, value_ref, prefix_ref, *refs):
    high_out, low_out, local_out, high_own, low_own = refs
    groups, tokens, _ = query_ref.shape
    levels = weight_ref.shape[0]
    ahead = lax.broadcasted_iota(jnp.int32, (LANES, LANES), 0) <= lax.broadcasted_iota(
        jnp.int32, (LANES, LANES), 1
    )
    spots = [(group, chunk) for group in range(groups) for chunk in range(tokens // CHUNK)]

    def prepare(index):
        group, chunk = spots[index]
        rows = pl.ds(chunk * CHUNK, CHUNK)
        query = query_ref[group, rows, :].T
        high_own[index % 2], low_own[index % 2] = halves(
            query * token_row(weight_ref.at[0, group], chunk)
        )
        for level in range(1, levels):
            high, low = halves(query * token_row(weight_ref.at[level, group], chunk))
            high_out[group, pl.ds((level - 1) * DH, DH), rows] = high
            low_out[group, pl.ds((level - 1) * DH, DH), rows] = low

    prepare(0)
    for index, (group, chunk) in enumerate(spots):
        if index + 1 < len(spots):
            prepare(index + 1)
        rows = pl.ds(chunk * CHUNK, CHUNK)
        high, low = high_own[index % 2], low_own[index % 2]
        prefix = jnp.concatenate(halves(prefix_ref[group, chunk]), axis=1)
        left = jnp.concatenate([key_ref[group, rows, :], prefix], axis=0)
        mixed = dot(left, jnp.concatenate([high, high], axis=0)) + dot(left[:, :DH], low)
        scores_high, scores_low = causal_halves(mixed[:CHUNK], ahead)
        values = value_ref[group, :, rows]
        near = dot(values, scores_high)
        near = near[:DH] + near[DH:] + dot(values[:DH], scores_low)
        local_out[group, :, rows] = near + mixed[CHUNK:]


def combine_kernel(
    heads, local_ref, high_ref, low_ref, scaled_ref, *refs
):
    *bucket_refs, combined_out, sums_out = refs
    groups, _, tokens = local_ref.shape
    seq_index = lax.axis_index("seq")
    per = CHUNK // LANES
    for group in range(groups):
        buckets = []
        for level, bucket_ref in enumerate(bucket_refs):
            reads = seq_index >> level & 1
            buckets.append(jnp.where(reads == 1, bucket_ref[group], 0.0))
        bucket_high, bucket_low = halves(jnp.concatenate(buckets, axis=1))
        both = jnp.concatenate([bucket_high, bucket_low], axis=0)
        for chunk in range(tokens // CHUNK):
            rows = pl.ds(chunk * CHUNK, CHUNK)
            square = dot(both, high_ref[group, :, rows])
            square = square[:DH] + square[DH:] + dot(bucket_high, low_ref[group, :, rows])
            combined = square + local_ref[group, :, rows]
            combined_out[group, :, rows] = combined
            sums = (
                jnp.sum(combined * combined, axis=0, keepdims=True),
                jnp.sum(combined * scaled_ref[group, :, rows], axis=0, keepdims=True),
            )
            for kind in range(2):
                for part in range(per):
                    spot = (kind, group // heads, pl.ds(chunk * per + part, 1))
                    row = sums[kind][:, part * LANES : (part + 1) * LANES]
                    sums_out[spot] = row if group % heads == 0 else sums_out[spot] + row


def factors(sums_ref, batch, full_width):
    inverse = lax.rsqrt(sums_ref[0, batch] / full_width + EPSILON)
    return inverse, inverse * inverse * inverse * sums_ref[1, batch] / full_width


def token_row(array, chunk):
    per = CHUNK // LANES
    spots = range(chunk * per, (chunk + 1) * per)
    return jnp.concatenate([array[spot : spot + 1, :] for spot in spots], axis=1)


def fold(total):
    total = total[:DH] + total[DH:]
    return (total[:, :DH] + total[:, DH:]).T


def top_gradient_kernel(
    heads, full_width, sums_ref, combined_ref, scaled_ref, high_ref, low_ref, *outs
):
    grad_out, parts_out = outs
    groups, _, tokens = combined_ref.shape
    level = high_ref.shape[1] // DH - 1
    top = pl.ds(level * DH, DH)
    reads = lax.axis_index("seq") >> level & 1
    for group in range(groups):
        inverse, pull = factors(sums_ref, group // heads, full_width)
        for chunk in range(tokens // CHUNK):
            rows = pl.ds(chunk * CHUNK, CHUNK)
            grad = scaled_ref[group, :, rows] * token_row(inverse, chunk) - combined_ref[
                group, :, rows
            ] * token_row(pull, chunk)
            parts_out[group, :, rows] = jnp.concatenate(halves(grad), axis=0)
        weighted = jnp.concatenate([high_ref[group, top, :], low_ref[group, top, :]], 0)
        total = dot(parts_out[group], weighted, NT)
        grad_out[group] = jnp.where(reads == 1, fold(total), 0.0)


def rest_gradient_kernel(parts_ref, high_ref, low_ref, *grad_outs):
    groups, _, _ = parts_ref.shape
    for level, grad_out in enumerate(grad_outs):
        spot = pl.ds(level * DH, DH)
        reads = lax.axis_index("seq") >> level & 1
        for group in range(groups):
            weighted = jnp.concatenate([high_ref[group, spot, :], low_ref[group, spot, :]], 0)
            total = dot(parts_ref[group], weighted, NT)
            grad_out[group] = jnp.where(reads == 1, fold(total), 0.0)


def finish_kernel(*refs):
    *part_refs, out_ref = refs
    total = part_refs[0][...]
    for part_ref in part_refs[1:]:
        total = total + part_ref[...]
    out_ref[...] = total


def attended_kernel(
    heads, full_width, sums_ref, combined_ref, gain_ref, attended_hbm, attended_ref, sems
):
    groups, _, tokens = combined_ref.shape
    copies = []
    for group in range(groups):
        gain = gain_ref[pl.ds(group % heads, 1), :]
        inverse, _ = factors(sums_ref, group // heads, full_width)
        for chunk in range(tokens // CHUNK):
            rows = pl.ds(chunk * CHUNK, CHUNK)
            scaled = combined_ref[group, :, rows] * token_row(inverse, chunk)
            attended_ref[group, rows, :] = scaled.T * gain
            if (chunk + 1) * CHUNK % LOAD == 0:
                load = (chunk + 1) * CHUNK // LOAD - 1
                rows = pl.ds(load * LOAD, LOAD)
                copies.append(
                    pltpu.make_async_copy(
                        attended_ref.at[group, rows],
                        attended_hbm.at[group, rows],
                        sems.at[group, load],
                    )
                )
                copies[-1].start()
    for copy in copies:
        copy.wait()


def resident(shape, dtype=F32):
    return pltpu.VMEM(shape, dtype)


def keep(array):
    return pltpu.with_memory_space_constraint(array, pltpu.VMEM)


def leave(array):
    return pltpu.with_memory_space_constraint(array, pltpu.HBM)


def partner(shard, axis, stride):
    return lax.ppermute(shard, axis, [(i, i ^ 1 << stride) for i in range(lax.axis_size(axis))])


def exchange(shard, axis, masks):
    size = lax.axis_size(axis)
    others = [lax.ppermute(shard, axis, [(i, i ^ mask) for i in range(size)]) for mask in masks]
    return sum(others, shard)


def body(
    query_rows, key_rows, value_rows, cotangent, selector, level_table, span_length, norm_gain
):
    batch_count, tokens, local_width = query_rows.shape
    heads = local_width // DH
    groups = batch_count * heads
    full_width = local_width * lax.axis_size("head")
    level_count = lax.axis_size("seq").bit_length() - 1

    def split(rows):
        rows = rows.reshape(batch_count, tokens, heads, DH)
        return rows.transpose(0, 2, 1, 3).reshape(groups, tokens, DH)

    queries, keys, values, cotangents = map(split, (query_rows, key_rows, value_rows, cotangent))
    selectors = selector.reshape(groups, tokens // LANES, LANES)
    gains = norm_gain.reshape(heads, DH)
    chunks = tokens // CHUNK
    stacked = level_count * DH
    call = functools.partial(
        pl.pallas_call, compiler_params=pltpu.CompilerParams(vmem_limit_bytes=GRANT)
    )

    key_parts, value_parts, prefixes, state, weights = call(
        functools.partial(state_kernel, heads),
        out_shape=(
            resident((groups, tokens, 2 * DH), BF16),
            resident((groups, 2 * DH, tokens), BF16),
            resident((groups, chunks, DH, DH)),
            resident((groups, DH, DH)),
            resident((level_count + 1, groups, tokens // LANES, LANES)),
        ),
        in_specs=[HBM] * 5,
        out_specs=(VMEM,) * 5,
        scratch_shapes=[
            pltpu.SMEM((batch_count,), jnp.int32),
            pltpu.SMEM(level_table.shape[::-1], F32),
            pltpu.VMEM(selectors.shape, jnp.int32),
            pltpu.VMEM((groups, tokens, DH), F32),
            pltpu.VMEM((groups, tokens, DH), F32),
            pltpu.SemaphoreType.DMA((3,)),
            pltpu.SemaphoreType.DMA((2, groups, tokens // LOAD)),
        ],
        name="state",
        compiler_params=pltpu.CompilerParams(vmem_limit_bytes=GRANT),
    )(
        *map(
            leave,
            (span_length.reshape(batch_count), level_table.T, selectors, keys, values),
        )
    )
    state, queries, cotangents, gains = lax.optimization_barrier(
        (state, queries, cotangents, gains)
    )

    buckets = []
    for level in reversed(range(level_count)):
        bucket = partner(state, "seq", level)
        for lower in reversed(range(level)):
            bucket = bucket + partner(bucket, "seq", lower)
        buckets.insert(0, bucket)

    weighted_high, weighted_low, local_sum = call(
        local_kernel,
        out_shape=(
            resident((groups, stacked, tokens), BF16),
            resident((groups, stacked, tokens), BF16),
            resident((groups, DH, tokens)),
        ),
        in_specs=[VMEM] * 5,
        out_specs=(VMEM,) * 3,
        scratch_shapes=[pltpu.VMEM((2, DH, CHUNK), BF16)] * 2,
        name="local",
        compiler_params=pltpu.CompilerParams(vmem_limit_bytes=GRANT),
    )(*map(keep, (weights, queries, key_parts, value_parts, prefixes)))

    scaled = call(
        functools.partial(scale_kernel, heads),
        out_shape=resident((groups, DH, tokens)),
        in_specs=[VMEM] * 2,
        out_specs=VMEM,
        name="scale",
    )(cotangents, gains)

    combined, sums = call(
        functools.partial(combine_kernel, heads),
        out_shape=(
            resident((groups, DH, tokens)),
            resident((2, batch_count, tokens // LANES, LANES)),
        ),
        in_specs=[VMEM] * (4 + level_count),
        out_specs=(VMEM,) * 2,
        name="combine",
    )(*map(keep, (local_sum, weighted_high, weighted_low, scaled, *buckets)))

    head_bits = lax.axis_size("head").bit_length() - 1
    rounds = [(1 << level,) for level in reversed(range(2, head_bits))]
    rounds += [(1, 3, 2)[: (1 << min(2, head_bits)) - 1]]
    for masks in rounds:
        sums = exchange(sums, "head", masks)

    top_grad, grad_parts = call(
        functools.partial(top_gradient_kernel, heads, full_width),
        out_shape=(resident((groups, DH, DH)), resident((groups, 2 * DH, tokens), BF16)),
        in_specs=[VMEM] * 5,
        out_specs=(VMEM,) * 2,
        name="top_gradient",
    )(*map(keep, (sums, combined, scaled, weighted_high, weighted_low)))
    grads = call(
        rest_gradient_kernel,
        out_shape=(resident((groups, DH, DH)),) * (level_count - 1),
        in_specs=[VMEM] * 3,
        out_specs=(VMEM,) * (level_count - 1),
        name="rest_gradient",
    )(*map(keep, (grad_parts, weighted_high, weighted_low)))

    attended = call(
        functools.partial(attended_kernel, heads, full_width),
        out_shape=jax.ShapeDtypeStruct((groups, tokens, DH), F32),
        in_specs=[VMEM] * 3,
        out_specs=HBM,
        scratch_shapes=[
            pltpu.VMEM((groups, tokens, DH), F32),
            pltpu.SemaphoreType.DMA((groups, tokens // LOAD)),
        ],
        name="attended",
    )(keep(sums), keep(combined), gains)

    total = partner(top_grad, "seq", level_count - 1)
    parts = []
    for level in reversed(range(level_count - 1)):
        total = sum(parts, total)
        received = partner(grads[level], "seq", level)
        parts = [partner(total, "seq", level), received]
    total = call(
        finish_kernel,
        out_shape=jax.ShapeDtypeStruct((groups, DH, DH), F32),
        in_specs=[VMEM] * 3,
        out_specs=VMEM,
        name="finish",
    )(*map(keep, (total, *parts)))

    def merge(rows, count):
        rows = rows.reshape(batch_count, heads, count, DH)
        return rows.transpose(0, 2, 1, 3).reshape(batch_count, count, heads * DH)

    return merge(attended, tokens), merge(total, DH)[:, None]


def solution(mesh):
    return jax.shard_map(
        body,
        mesh=mesh,
        in_specs=(
            P(None, "seq", "head"),
            P(None, "seq", "head"),
            P(None, "seq", "head"),
            P(None, "seq", "head"),
            P(None, "head", "seq"),
            P(),
            P(None, "seq"),
            P("head"),
        ),
        out_specs=(P(None, "seq", "head"), P(None, "seq", None, "head")),
        check_vma=False,
    )
```
